256 devices in a mesh: layer: 8 (over x_lo, y), dp: 32 (over z, x_hi, core).
Axes of the slice: x: 4 (x_hi: 2, x_lo: 2; x = x_hi * 2 + x_lo), y: 4, z: 8, core: 2. Of those that a mesh axis runs over, the one named last changes fastest.
Arguments:
- states: bfloat16 [16, 64, 32, 32, 256], P('layer', 'dp'), may hold values from -6 to 6
- slopes: bfloat16 [16, 64, 32, 32, 256], P('layer', 'dp'), may hold values from 0.099609375 to 1
- kernels: bfloat16 [16, 9, 256, 256], P('layer'), may hold values from -0.125 to 0.125
- guess: float32 [16, 64, 32, 32, 256], P('layer', 'dp'), may hold values from -6 to 6
Outputs:
- lower_adjoint: float32 [8, 64, 32, 32, 256], P('layer', 'dp')
- kernel_grad: float32 [16, 9, 256, 256], P('layer', None, 'dp')
The draws below stay inside these ranges and needn't reach their ends.
All inputs are finite; a program needn't handle non-finite values.
Results may differ from the reference program's by a relative error of at most 0.005.
Values sent between devices are 32-bit elements; how exact they have to be, the bound alone decides.
A program may use at most 64 MiB of HBM per device.

```python
import jax
import jax.numpy as jnp

C = 256
HEIGHT = 32
WIDTH = 32
L_DEV = 2
IMAGES = 64
LAYERS = 16
N_LAYER = 8


def with_spikes(array, own_key, source, target, blocks, factor):
    owner, partner = [(jnp.arange(array.shape[dim]) // (array.shape[dim] // blocks)).reshape([-1 if axis == dim else 1 for axis in range(array.ndim)]) for dim in (source, target)]
    chosen = jax.random.permutation(own_key, blocks)[partner]
    strong = (owner == chosen) | (owner == (partner + blocks // 2) % blocks)
    return jnp.where(strong, factor * array, array)


def level_of(own_key, shape, split, smallest, largest):
    def one(dim, blocks):
        steps = jax.random.uniform(jax.random.fold_in(jax.random.fold_in(own_key, 6), dim), (blocks,), jnp.float32, smallest / len(split), largest / len(split))
        return jnp.repeat(jnp.exp(steps), shape[dim] // blocks).reshape((-1,) + (1,) * (len(shape) - dim - 1))

    factor_of = one(*split[0])
    for cut in split[1:]:
        factor_of = factor_of * one(*cut)
    return factor_of


def scatter_about(rng, shape, deviation, most, cuts=(), dtype=jnp.bfloat16):
    array = deviation * jax.random.normal(rng, shape, jnp.float32)
    if cuts:
        array = array * level_of(rng, shape, cuts, -0.22, 0.18)
    return jnp.clip(array, -most, most).astype(dtype)


def heavy_noise(stream_key, shape, spread, reach, cuts, heavy, dtype=jnp.bfloat16):
    entries = spread * jax.random.normal(stream_key, shape, jnp.float32)
    if cuts:
        entries = entries * level_of(stream_key, shape, cuts, -0.22, 0.18)
    return jnp.clip(with_spikes(entries, jax.random.fold_in(stream_key, 3), *heavy), -reach, reach).astype(dtype)


def setup_inputs(seed: int = 0) -> dict:
    streams_of = jax.random.split(jax.random.key(seed), 5)
    states = heavy_noise(streams_of[0], (LAYERS, IMAGES, HEIGHT, WIDTH, C), 1.0, 6.0, ((0, 8), (1, 32)), (1, 4, 32, 2.75))
    slopes = jnp.clip(0.099609375 + 0.9003906 * jax.random.uniform(streams_of[1], (LAYERS, IMAGES, HEIGHT, WIDTH, C), jnp.float32) ** level_of(streams_of[1], (LAYERS, IMAGES, HEIGHT, WIDTH, C), ((0, 8), (1, 32)), -0.2, 0.2), 0.099609375, 1.0).astype(jnp.bfloat16)
    kernels = scatter_about(streams_of[2], (LAYERS, 9, C, C), (9 * C) ** -0.5, 0.125, ((0, 8),))
    guess = scatter_about(streams_of[3], (LAYERS, IMAGES, HEIGHT, WIDTH, C), 1.0, 6.0, ((0, 8), (1, 32)), jnp.float32)
    return {"states": states, "slopes": slopes, "kernels": kernels, "guess": guess}


step_size = 0.5


def padded_float(images):
    return jnp.pad(images.astype(jnp.float32), ((0, 0), (1, 1), (1, 1), (0, 0)))


def transpose_conv(cotangent, kernel):
    image_count = cotangent.shape[0]
    image_height = cotangent.shape[1]
    image_width = cotangent.shape[2]
    channels = cotangent.shape[3]
    padded = padded_float(cotangent)
    kernel_float = kernel.astype(jnp.float32)
    total = jnp.zeros((image_count * image_height * image_width, channels), jnp.float32)
    for row_shift in range(3):
        for col_shift in range(3):
            piece = padded[:, 2 - row_shift:2 - row_shift + image_height, 2 - col_shift:2 - col_shift + image_width, :]
            piece = piece.reshape(image_count * image_height * image_width, channels)
            total = total + jnp.dot(piece, kernel_float[3 * row_shift + col_shift].T, preferred_element_type=jnp.float32)
    return total.reshape(cotangent.shape)


def correlate(inputs, cotangent):
    image_count = inputs.shape[0]
    image_height = inputs.shape[1]
    image_width = inputs.shape[2]
    channels = inputs.shape[3]
    padded = padded_float(inputs)
    rows = image_count * image_height * image_width
    cot_rows = cotangent.astype(jnp.float32).reshape(rows, channels)
    taps = []
    for row_shift in range(3):
        for col_shift in range(3):
            piece = padded[:, row_shift:row_shift + image_height, col_shift:col_shift + image_width, :].reshape(rows, channels)
            taps.append(jnp.dot(piece.T, cot_rows, preferred_element_type=jnp.float32))
    return jnp.stack(taps)


def apply_layer(adjoint, slope, kernel, factor):
    cotangent = (slope.astype(jnp.float32) * adjoint).astype(jnp.bfloat16)
    return adjoint + factor * transpose_conv(cotangent, kernel), cotangent


def reference(states, slopes, kernels, guess):
    sections = N_LAYER
    layer_count = L_DEV
    images = states.shape[1]
    carried = [jnp.zeros(guess.shape[1:], jnp.float32) for section in range(sections)]
    following = jnp.zeros(guess.shape[1:], jnp.float32)
    for section in range(sections - 1, 0, -1):
        bottom = section * layer_count
        section_end, unused = apply_layer(guess[bottom], slopes[bottom], kernels[bottom], step_size)
        coarse, unused = apply_layer(following, slopes[bottom], kernels[bottom], step_size * layer_count)
        following = (coarse + section_end) - guess[bottom - 1]
        carried[section - 1] = following
    lowers = []
    gradients = [None] * (sections * layer_count)
    for section in range(sections):
        adjoint = guess[section * layer_count + layer_count - 1] + carried[section]
        for inner_layer in range(layer_count - 1, -1, -1):
            layer_index = section * layer_count + inner_layer
            adjoint, cotangent = apply_layer(adjoint, slopes[layer_index], kernels[layer_index], step_size)
            gradients[layer_index] = correlate(states[layer_index], cotangent) * (step_size / images)
        lowers.append(adjoint)
    return jnp.stack(lowers), jnp.stack(gradients)
```

```python
import functools

import jax
import jax.numpy as jnp
from jax import lax
from jax.experimental import pallas as pl
from jax.experimental.pallas import tpu as pltpu
from jax.sharding import PartitionSpec as P

MESH = pl.DeviceIdType.MESH
STEP = 0.5
TOP = 8
ROWS = 88
R = 2
Q = 4
BLK = R * Q


def chain_kernel(
    sections, scale, height, width, chans,
    states_hbm, slopes_hbm, kernels_hbm, guess_hbm,
    lower_hbm, grad_hbm,
    states, slopes, kern, last, ends, recv, send, mid, low, z_chain, z_up, z_dn, grad,
    load_sems, send_sems, recv_sems, out_sems,
):
    s = lax.axis_index("layer")
    h = sections - 1 - s
    pix = height * width
    image_row = (1, height + 2)
    end_row = 2 * height + 1

    def rows(start, count):
        return pl.ds(pl.multiple_of((start + TOP) * width, width), count * width)

    def image(ref, i):
        return ref.at[rows(image_row[i], height)]

    def load(src, dst, sem):
        copy = pltpu.make_async_copy(src, dst, sem)
        copy.start()
        return copy

    pads = ((-TOP, TOP + 1), (height + 1, 1), (end_row + 1, ROWS - TOP - end_row - 1))

    def clear(ref):
        for start, count in pads:
            part = ref.at[rows(start, count)]
            part[...] = jnp.zeros(part.shape, part.dtype)

    first = [load(kernels_hbm.at[0], kern.at[0], load_sems.at[0])]
    for i in range(2):
        first.append(load(guess_hbm.at[0, i], image(ends, i), load_sems.at[1 + i]))
        first.append(load(slopes_hbm.at[0, i], image(slopes.at[0], i), load_sems.at[3 + i]))
    rest = [load(kernels_hbm.at[1], kern.at[1], load_sems.at[5])]
    for i in range(2):
        rest.append(load(guess_hbm.at[1, i], image(last, i), load_sems.at[6 + i]))
        rest.append(load(slopes_hbm.at[1, i], image(slopes.at[1], i), load_sems.at[8 + i]))
        for l in range(2):
            rest.append(load(states_hbm.at[l, i], image(states.at[l], i), load_sems.at[10 + 2 * l + i]))

    clear(recv)
    barrier = pltpu.get_barrier_semaphore()

    @pl.when(s > 0)
    def _():
        pl.semaphore_signal(barrier, inc=1, device_id={"layer": s - 1}, device_id_type=MESH)

    @pl.when(s < sections - 1)
    def _():
        pl.semaphore_signal(barrier, inc=1, device_id={"layer": s + 1}, device_id_type=MESH)

    clear(ends)
    clear(last)
    clear(slopes.at[0])
    clear(slopes.at[1])
    clear(states.at[0])
    clear(states.at[1])
    for ref in (z_chain, z_up, z_dn):
        clear(ref)
    z_up[rows(-TOP, TOP + 4)] = jnp.zeros(((TOP + 4) * width, 3 * chans), jnp.bfloat16)
    z_dn[rows(-TOP, TOP + 4)] = jnp.zeros(((TOP + 4) * width, 3 * chans), jnp.bfloat16)
    grad[...] = jnp.zeros(grad.shape, jnp.float32)

    for copy in first:
        copy.wait()

    def spread(z, start, count, slope, values):
        cot = slope.astype(jnp.float32) * values
        size = count * width
        col = lax.broadcasted_iota(jnp.int32, (size, chans), 0) % width
        z[rows(start, count), chans:2 * chans] = cot.astype(jnp.bfloat16)
        ahead = jnp.where(col == width - 1, 0.0, pltpu.roll(cot, size - 1, 0))
        z[rows(start, count), 0:chans] = ahead.astype(jnp.bfloat16)
        behind = jnp.where(col == 0, 0.0, pltpu.roll(cot, 1, 0))
        z[rows(start, count), 2 * chans:3 * chans] = behind.astype(jnp.bfloat16)

    def conv(z, layer, start, count):
        total = None
        for a in range(3):
            for b in range(3):
                piece = z[rows(start + 1 - a, count), b * chans:(b + 1) * chans]
                term = lax.dot_general(
                    piece, kern[layer, 3 * a + b], (((1,), (1,)), ((), ())),
                    preferred_element_type=jnp.float32,
                )
                total = term if total is None else total + term
        return total

    def sends(k, hop):
        start = R * k + 1 - hop
        return (start + R - 1 >= 1) & (start <= end_row)

    def chunk(src, k):
        where = rows(R * k + 1 - h, R)
        return pltpu.make_async_remote_copy(
            src_ref=src.at[where],
            dst_ref=recv.at[where],
            send_sem=send_sems.at[k],
            recv_sem=recv_sems.at[k],
            device_id={"layer": s - 1},
            device_id_type=MESH,
        )

    def arrival(k):
        where = rows(R * k + 2 - h, R)
        return pltpu.make_async_remote_copy(
            src_ref=recv.at[where],
            dst_ref=recv.at[where],
            send_sem=send_sems.at[k],
            recv_sem=recv_sems.at[k],
            device_id={"layer": s - 1},
            device_id_type=MESH,
        )

    pl.semaphore_wait(barrier, jnp.where(s > 0, 1, 0) + jnp.where(s < sections - 1, 1, 0))

    def spread_end(j):
        at = rows(BLK * j, BLK)
        spread(z_chain, BLK * j, BLK, slopes[0, at], ends[at])

    blocks = -(-(end_row + 1) // BLK)
    spread_end(0)

    @pl.loop(0, blocks)
    def _(j):
        @pl.when(j < blocks - 1)
        def _():
            spread_end(j + 1)

        at = rows(BLK * j, BLK)
        ends[at] = ends[at] + STEP * conv(z_chain, 0, BLK * j, BLK)

        @pl.when(h == 0)
        def _():
            for q in range(Q):
                k = Q * j - 1 + q

                @pl.when((k >= 0) & sends(k, 0))
                def _():
                    chunk(ends, k).start()

    for copy in rest:
        copy.wait()

    @pl.when(h == 0)
    def _():
        for i in range(2):
            at = rows(image_row[i], height)
            recv[at] = last[at]

    def fine(j, piece):
        start = BLK * (j - 1) + 2 - jnp.maximum(h, 1)

        def gradient(layer, z, at):
            lhs = jnp.concatenate(
                [states[layer, rows(at + a - 1, BLK)].T for a in range(3)], axis=0
            )
            for b in range(3):
                term = jnp.dot(lhs, z[rows(at, BLK), b * chans:(b + 1) * chans],
                               preferred_element_type=jnp.float32)
                for a in range(3):
                    grad[layer, 3 * a + b] += term[a * chans:(a + 1) * chans]

        if piece == 0:
            at = rows(start, BLK)
            spread(z_up, start, BLK, slopes[1, at], recv[at])
            at = rows(start - 1, BLK)
            mid[at] = recv[at] + STEP * conv(z_up, 1, start - 1, BLK)
        elif piece == 1:
            at = rows(start - 1, BLK)
            spread(z_dn, start - 1, BLK, slopes[0, at], mid[at])
            at = rows(start - 2, BLK + 1)
            low[at] = mid[at] + STEP * conv(z_dn, 0, start - 2, BLK + 1)
        elif piece == 2:
            gradient(1, z_up, start)
        else:
            gradient(0, z_dn, start - 1)

    outer = -(-(end_row + sections - 2) // BLK)

    @pl.loop(0, outer)
    def _(j):
        for q in range(Q):
            k = Q * j + q
            taken = (h > 0) & sends(k, h - 1)

            @pl.when(taken)
            def _():
                arrival(k).wait_recv()

            @pl.when(taken & (s > 0))
            def _():
                at = rows(R * k + 2 - h, R)
                spread(z_chain, R * k + 2 - h, R, slopes[0, at], recv[at] - last[at])

            @pl.when((h > 0) & (s > 0) & sends(k, h))
            def _():
                at = rows(R * k + 1 - h, R)
                send[at] = ((recv[at] - last[at]) + 2 * STEP * conv(z_chain, 0, R * k + 1 - h, R)) + ends[at]
                chunk(send, k).start()

            @pl.when(j > 0)
            def _():
                fine(j, q)

    for piece in range(4):
        fine(outer, piece)

    grad[...] = grad[...] * scale
    outs = [load(image(low, i), lower_hbm.at[i], out_sems.at[i]) for i in range(2)]
    outs.append(load(grad, grad_hbm, out_sems.at[2]))

    @pl.loop(0, outer * Q)
    def _(k):
        @pl.when((s > 0) & sends(k, h))
        def _():
            chunk(send, k).wait_send()

    for copy in outs:
        copy.wait()


def on_device(states, slopes, kernels, guess):
    layers, images, height, width, chans = states.shape
    sections = lax.axis_size("layer")
    replicas = lax.axis_size("dp")
    scale = STEP / (images * replicas)
    pix = height * width
    flat = lambda array: array.reshape(layers, images, pix, chans)
    steps = Q * -(-(2 * height + 1 + sections - 2) // BLK)
    size = ROWS * width
    any_space = pl.BlockSpec(memory_space=pl.ANY)
    f32, bf16 = jnp.float32, jnp.bfloat16
    lower, grads = pl.pallas_call(
        functools.partial(chain_kernel, sections, scale, height, width, chans),
        out_shape=(
            jax.ShapeDtypeStruct((images, pix, chans), f32),
            jax.ShapeDtypeStruct((layers, 9, chans, chans), f32),
        ),
        in_specs=[any_space] * 4,
        out_specs=(any_space, any_space),
        scratch_shapes=[
            pltpu.VMEM((layers, size, chans), bf16),
            pltpu.VMEM((layers, size, chans), bf16),
            pltpu.VMEM((layers, 9, chans, chans), bf16),
            pltpu.VMEM((size, chans), f32),
            pltpu.VMEM((size, chans), f32),
            pltpu.VMEM((size, chans), f32),
            pltpu.VMEM((size, chans), f32),
            pltpu.VMEM((size, chans), f32),
            pltpu.VMEM((size, chans), f32),
            pltpu.VMEM((size, 3 * chans), bf16),
            pltpu.VMEM((size, 3 * chans), bf16),
            pltpu.VMEM((size, 3 * chans), bf16),
            pltpu.VMEM((layers, 9, chans, chans), f32),
            pltpu.SemaphoreType.DMA((14,)),
            pltpu.SemaphoreType.DMA((steps,)),
            pltpu.SemaphoreType.DMA((steps,)),
            pltpu.SemaphoreType.DMA((3,)),
        ],
        compiler_params=pltpu.CompilerParams(
            collective_id=0, has_side_effects=True, vmem_limit_bytes=60 * 1024 * 1024
        ),
    )(flat(states), flat(slopes), kernels, flat(guess))
    summed = lax.psum_scatter(grads, "dp", scatter_dimension=2, tiled=True)
    return (lower.reshape(1, images, height, width, chans), summed)


def solution(mesh):
    return jax.shard_map(
        on_device,
        mesh=mesh,
        in_specs=(
            P("layer", "dp", None, None, None),
            P("layer", "dp", None, None, None),
            P("layer", None, None, None),
            P("layer", "dp", None, None, None),
        ),
        out_specs=(P("layer", "dp", None, None, None), P("layer", None, "dp", None)),
        check_vma=False,
    )
```

```python
import functools

import jax
import jax.numpy as jnp
from jax import lax
from jax.experimental import pallas as pl
from jax.experimental.pallas import tpu as pltpu
from jax.sharding import PartitionSpec as P

MESH = pl.DeviceIdType.MESH
STEP = 0.5
TOP = 8
ROWS = 88
R = 2
Q = 4
BLK = R * Q
PART = 6


def chain_kernel(
    sections, scale, height, width, chans,
    states_hbm, slopes_hbm, kernels_hbm, guess_hbm,
    lower_hbm, grad_hbm,
    states, slopes, kern, last, ends, recv, send, mid, low, z_chain, z_up, z_dn, grad,
    core_in, ring_in, cross_in, result,
    load_sems, send_sems, recv_sems, out_sems,
    core_sems, ring_send, ring_recv, cross_sems,
):
    s = lax.axis_index("layer")
    h = sections - 1 - s
    pix = height * width
    image_row = (1, height + 2)
    end_row = 2 * height + 1

    def rows(start, count):
        return pl.ds(pl.multiple_of((start + TOP) * width, width), count * width)

    def image(ref, i):
        return ref.at[rows(image_row[i], height)]

    def load(src, dst, sem):
        copy = pltpu.make_async_copy(src, dst, sem)
        copy.start()
        return copy

    pads = ((-TOP, TOP + 1), (height + 1, 1), (end_row + 1, ROWS - TOP - end_row - 1))

    def clear(ref):
        for start, count in pads:
            part = ref.at[rows(start, count)]
            part[...] = jnp.zeros(part.shape, part.dtype)

    first = [load(kernels_hbm.at[0], kern.at[0], load_sems.at[0])]
    for i in range(2):
        first.append(load(guess_hbm.at[0, i], image(ends, i), load_sems.at[1 + i]))
        first.append(load(slopes_hbm.at[0, i], image(slopes.at[0], i), load_sems.at[3 + i]))
    rest = [load(kernels_hbm.at[1], kern.at[1], load_sems.at[5])]
    for i in range(2):
        rest.append(load(guess_hbm.at[1, i], image(last, i), load_sems.at[6 + i]))
        rest.append(load(slopes_hbm.at[1, i], image(slopes.at[1], i), load_sems.at[8 + i]))
        for l in range(2):
            rest.append(load(states_hbm.at[l, i], image(states.at[l], i), load_sems.at[10 + 2 * l + i]))

    place = lax.axis_index("dp")
    ring = lax.axis_size("dp") // 4
    depth = place // 4
    cross = (place // 2) % 2
    core = place % 2
    beside = place + 1 - 2 * core
    over = place + 2 - 4 * cross
    after = ((depth + 1) % ring) * 4 + place % 4
    before = ((depth + ring - 1) % ring) * 4 + place % 4

    clear(recv)
    barrier = pltpu.get_barrier_semaphore()
    for peer in (beside, over, after, before):
        pl.semaphore_signal(barrier, inc=1, device_id={"dp": peer}, device_id_type=MESH)

    @pl.when(s > 0)
    def _():
        pl.semaphore_signal(barrier, inc=1, device_id={"layer": s - 1}, device_id_type=MESH)

    @pl.when(s < sections - 1)
    def _():
        pl.semaphore_signal(barrier, inc=1, device_id={"layer": s + 1}, device_id_type=MESH)

    clear(ends)
    clear(last)
    clear(slopes.at[0])
    clear(slopes.at[1])
    clear(states.at[0])
    clear(states.at[1])
    for ref in (z_chain, z_up, z_dn):
        clear(ref)
    z_up[rows(-TOP, TOP + 4)] = jnp.zeros(((TOP + 4) * width, 3 * chans), jnp.bfloat16)
    z_dn[rows(-TOP, TOP + 4)] = jnp.zeros(((TOP + 4) * width, 3 * chans), jnp.bfloat16)
    grad[...] = jnp.zeros(grad.shape, jnp.float32)

    for copy in first:
        copy.wait()

    def spread(z, start, count, slope, values):
        cot = slope.astype(jnp.float32) * values
        size = count * width
        col = lax.broadcasted_iota(jnp.int32, (size, chans), 0) % width
        z[rows(start, count), chans:2 * chans] = cot.astype(jnp.bfloat16)
        ahead = jnp.where(col == width - 1, 0.0, pltpu.roll(cot, size - 1, 0))
        z[rows(start, count), 0:chans] = ahead.astype(jnp.bfloat16)
        behind = jnp.where(col == 0, 0.0, pltpu.roll(cot, 1, 0))
        z[rows(start, count), 2 * chans:3 * chans] = behind.astype(jnp.bfloat16)

    def conv(z, layer, start, count):
        total = None
        for a in range(3):
            for b in range(3):
                piece = z[rows(start + 1 - a, count), b * chans:(b + 1) * chans]
                term = lax.dot_general(
                    piece, kern[layer, 3 * a + b], (((1,), (1,)), ((), ())),
                    preferred_element_type=jnp.float32,
                )
                total = term if total is None else total + term
        return total

    def sends(k, hop):
        start = R * k + 1 - hop
        return (start + R - 1 >= 1) & (start <= end_row)

    def chunk(src, k):
        where = rows(R * k + 1 - h, R)
        return pltpu.make_async_remote_copy(
            src_ref=src.at[where],
            dst_ref=recv.at[where],
            send_sem=send_sems.at[k],
            recv_sem=recv_sems.at[k],
            device_id={"layer": s - 1},
            device_id_type=MESH,
        )

    def arrival(k):
        where = rows(R * k + 2 - h, R)
        return pltpu.make_async_remote_copy(
            src_ref=recv.at[where],
            dst_ref=recv.at[where],
            send_sem=send_sems.at[k],
            recv_sem=recv_sems.at[k],
            device_id={"layer": s - 1},
            device_id_type=MESH,
        )

    pl.semaphore_wait(barrier, 4 + jnp.where(s > 0, 1, 0) + jnp.where(s < sections - 1, 1, 0))

    def spread_end(j):
        at = rows(BLK * j, BLK)
        spread(z_chain, BLK * j, BLK, slopes[0, at], ends[at])

    blocks = -(-(end_row + 1) // BLK)
    spread_end(0)

    @pl.loop(0, blocks)
    def _(j):
        @pl.when(j < blocks - 1)
        def _():
            spread_end(j + 1)

        at = rows(BLK * j, BLK)
        ends[at] = ends[at] + STEP * conv(z_chain, 0, BLK * j, BLK)

        @pl.when(h == 0)
        def _():
            for q in range(Q):
                k = Q * j - 1 + q

                @pl.when((k >= 0) & sends(k, 0))
                def _():
                    chunk(ends, k).start()

    for copy in rest:
        copy.wait()

    @pl.when(h == 0)
    def _():
        for i in range(2):
            at = rows(image_row[i], height)
            recv[at] = last[at]

    def fine(j, piece):
        start = BLK * (j - 1) + 2 - jnp.maximum(h, 1)

        def gradient(layer, z, at):
            lhs = jnp.concatenate(
                [states[layer, rows(at + a - 1, BLK)].T for a in range(3)], axis=0
            )
            for b in range(3):
                term = jnp.dot(lhs, z[rows(at, BLK), b * chans:(b + 1) * chans],
                               preferred_element_type=jnp.float32)
                for a in range(3):
                    part = term[a * chans:(a + 1) * chans]
                    grad[9 * layer + 3 * a + b] += part.reshape(grad.shape[1:])

        if piece == 0:
            at = rows(start, BLK)
            spread(z_up, start, BLK, slopes[1, at], recv[at])
            at = rows(start - 1, BLK)
            mid[at] = recv[at] + STEP * conv(z_up, 1, start - 1, BLK)
        elif piece == 1:
            at = rows(start - 1, BLK)
            spread(z_dn, start - 1, BLK, slopes[0, at], mid[at])
            at = rows(start - 2, BLK + 1)
            low[at] = mid[at] + STEP * conv(z_dn, 0, start - 2, BLK + 1)
        elif piece == 2:
            gradient(1, z_up, start)
        else:
            gradient(0, z_dn, start - 1)

    outer = -(-(end_row + sections - 2) // BLK)

    @pl.loop(0, outer)
    def _(j):
        for q in range(Q):
            k = Q * j + q
            taken = (h > 0) & sends(k, h - 1)

            @pl.when(taken)
            def _():
                arrival(k).wait_recv()

            @pl.when(taken & (s > 0))
            def _():
                at = rows(R * k + 2 - h, R)
                spread(z_chain, R * k + 2 - h, R, slopes[0, at], recv[at] - last[at])

            @pl.when((h > 0) & (s > 0) & sends(k, h))
            def _():
                at = rows(R * k + 1 - h, R)
                send[at] = ((recv[at] - last[at]) + 2 * STEP * conv(z_chain, 0, R * k + 1 - h, R)) + ends[at]
                chunk(send, k).start()

            @pl.when(j > 0)
            def _():
                fine(j, q)

    for piece in range(4):
        fine(outer, piece)

    outs = [load(image(low, i), lower_hbm.at[i], out_sems.at[i]) for i in range(2)]

    def remote(src, dst, send_sem, recv_sem, peer):
        return pltpu.make_async_remote_copy(
            src_ref=src, dst_ref=dst, send_sem=send_sem, recv_sem=recv_sem,
            device_id={"dp": peer}, device_id_type=MESH,
        )

    def part(u):
        return slice(PART * u, PART * (u + 1))

    parts = grad.shape[0] // PART
    half = ring // 2

    def core_copy(u):
        return remote(grad.at[part(u), :, :, 1 - core], core_in.at[part(u)],
                      core_sems.at[0, u], core_sems.at[1, u], beside)

    def ring_copy(way, j, u):
        away = half - j
        target = (depth + away) % ring if way == 0 else (depth + ring - away) % ring
        src, dst = grad.at[part(u), target, :, core], ring_in.at[way, j, part(u)]
        if j == 0:
            src, dst = src.at[:, way], dst.at[:, way]
        return remote(src, dst, ring_send.at[way, j, u], ring_recv.at[way, j, u],
                      after if way == 0 else before)

    def cross_copy(u):
        return remote(grad.at[part(u), depth, 1 - cross, core], cross_in.at[part(u)],
                      cross_sems.at[0, u], cross_sems.at[1, u], over)

    def add_arrived(way, j, u):
        ring_copy(way, j, u).wait_recv()
        away = half - 1 - j
        target = (depth + away) % ring if way == 0 else (depth + ring - away) % ring
        if j == 0:
            grad[part(u), target, way, core] += ring_in[way, j, part(u), way]
        else:
            grad[part(u), target, :, core] += ring_in[way, j, part(u)]

    for u in range(parts):
        core_copy(u).start()
    for u in range(parts):
        core_copy(u).wait_recv()
        grad[part(u), :, :, core] += core_in[part(u)]
        for way in range(2):
            ring_copy(way, 0, u).start()
    for j in range(1, half):
        for u in range(parts):
            for way in range(2):
                add_arrived(way, j - 1, u)
                ring_copy(way, j, u).start()
    for u in range(parts):
        for way in range(2):
            add_arrived(way, half - 1, u)
        cross_copy(u).start()
    for u in range(parts):
        cross_copy(u).wait_recv()
        result[part(u)] = (grad[part(u), depth, cross, core] + cross_in[part(u)]) * scale
    outs.append(load(result, grad_hbm, out_sems.at[2]))

    for u in range(parts):
        core_copy(u).wait_send()
        cross_copy(u).wait_send()
        for j in range(half):
            for way in range(2):
                ring_copy(way, j, u).wait_send()

    @pl.loop(0, outer * Q)
    def _(k):
        @pl.when((s > 0) & sends(k, h))
        def _():
            chunk(send, k).wait_send()

    for copy in outs:
        copy.wait()


def on_device(states, slopes, kernels, guess):
    layers, images, height, width, chans = states.shape
    sections = lax.axis_size("layer")
    replicas = lax.axis_size("dp")
    scale = STEP / (images * replicas)
    pix = height * width
    flat = lambda array: array.reshape(layers, images, pix, chans)
    steps = Q * -(-(2 * height + 1 + sections - 2) // BLK)
    size = ROWS * width
    any_space = pl.BlockSpec(memory_space=pl.ANY)
    f32, bf16 = jnp.float32, jnp.bfloat16
    ring = replicas // 4
    share = chans // replicas
    lower, grads = pl.pallas_call(
        functools.partial(chain_kernel, sections, scale, height, width, chans),
        out_shape=(
            jax.ShapeDtypeStruct((images, pix, chans), f32),
            jax.ShapeDtypeStruct((layers * 9, chans // replicas, chans), f32),
        ),
        in_specs=[any_space] * 4,
        out_specs=(any_space, any_space),
        scratch_shapes=[
            pltpu.VMEM((layers, size, chans), bf16),
            pltpu.VMEM((layers, size, chans), bf16),
            pltpu.VMEM((layers, 9, chans, chans), bf16),
            pltpu.VMEM((size, chans), f32),
            pltpu.VMEM((size, chans), f32),
            pltpu.VMEM((size, chans), f32),
            pltpu.VMEM((size, chans), f32),
            pltpu.VMEM((size, chans), f32),
            pltpu.VMEM((size, chans), f32),
            pltpu.VMEM((size, 3 * chans), bf16),
            pltpu.VMEM((size, 3 * chans), bf16),
            pltpu.VMEM((size, 3 * chans), bf16),
            pltpu.VMEM((layers * 9, ring, 2, 2, share, chans), f32),
            pltpu.VMEM((layers * 9, ring, 2, share, chans), f32),
            pltpu.VMEM((2, ring // 2, layers * 9, 2, share, chans), f32),
            pltpu.VMEM((layers * 9, share, chans), f32),
            pltpu.VMEM((layers * 9, share, chans), f32),
            pltpu.SemaphoreType.DMA((14,)),
            pltpu.SemaphoreType.DMA((steps,)),
            pltpu.SemaphoreType.DMA((steps,)),
            pltpu.SemaphoreType.DMA((3,)),
            pltpu.SemaphoreType.DMA((2, layers * 9 // PART)),
            pltpu.SemaphoreType.DMA((2, ring // 2, layers * 9 // PART)),
            pltpu.SemaphoreType.DMA((2, ring // 2, layers * 9 // PART)),
            pltpu.SemaphoreType.DMA((2, layers * 9 // PART)),
        ],
        compiler_params=pltpu.CompilerParams(
            collective_id=0, has_side_effects=True, vmem_limit_bytes=60 * 1024 * 1024
        ),
    )(flat(states), flat(slopes), kernels, flat(guess))
    return (
        lower.reshape(1, images, height, width, chans),
        grads.reshape(layers, 9, share, chans),
    )


def solution(mesh):
    return jax.shard_map(
        on_device,
        mesh=mesh,
        in_specs=(
            P("layer", "dp", None, None, None),
            P("layer", "dp", None, None, None),
            P("layer", None, None, None),
            P("layer", "dp", None, None, None),
        ),
        out_specs=(P("layer", "dp", None, None, None), P("layer", None, "dp", None)),
        check_vma=False,
    )
```

```python
import functools

import jax
import jax.numpy as jnp
from jax import lax
from jax.experimental import pallas as pl
from jax.experimental.pallas import tpu as pltpu
from jax.sharding import PartitionSpec as P

MESH = pl.DeviceIdType.MESH
STEP = 0.5
TOP = 8
ROWS = 88
R = 2
Q = 4
BLK = R * Q
PART = 3
RING_FIRST = (3, 0, 1, 2)
CROSS_FIRST = (4, 5)


def chain_kernel(
    sections, scale, height, width, chans,
    states_hbm, slopes_hbm, kernels_hbm, guess_hbm,
    lower_hbm, grad_hbm,
    states, slopes, kern, last, ends, recv, send, mid, low, z_chain, z_up, z_dn, grad,
    core_in, ring_in, cross_in, wide_in, result,
    load_sems, send_sems, recv_sems, out_sems,
    core_sems, ring_send, ring_recv, cross_sems,
):
    s = lax.axis_index("layer")
    h = sections - 1 - s
    pix = height * width
    image_row = (1, height + 2)
    end_row = 2 * height + 1

    def rows(start, count):
        return pl.ds(pl.multiple_of((start + TOP) * width, width), count * width)

    def image(ref, i):
        return ref.at[rows(image_row[i], height)]

    def load(src, dst, sem):
        copy = pltpu.make_async_copy(src, dst, sem)
        copy.start()
        return copy

    pads = ((-TOP, TOP + 1), (height + 1, 1), (end_row + 1, ROWS - TOP - end_row - 1))

    def clear(ref):
        for start, count in pads:
            part = ref.at[rows(start, count)]
            part[...] = jnp.zeros(part.shape, part.dtype)

    first = [load(kernels_hbm.at[0], kern.at[0], load_sems.at[0])]
    for i in range(2):
        first.append(load(guess_hbm.at[0, i], image(ends, i), load_sems.at[1 + i]))
        first.append(load(slopes_hbm.at[0, i], image(slopes.at[0], i), load_sems.at[3 + i]))
    place = lax.axis_index("dp")
    ring = lax.axis_size("dp") // 4
    depth = place // 4
    cross = (place // 2) % 2
    core = place % 2
    beside = place + 1 - 2 * core
    over = place + 2 - 4 * cross
    after = ((depth + 1) % ring) * 4 + place % 4
    before = ((depth + ring - 1) % ring) * 4 + place % 4

    clear(recv)
    barrier = pltpu.get_barrier_semaphore()
    for peer in (beside, over, after, before):
        pl.semaphore_signal(barrier, inc=1, device_id={"dp": peer}, device_id_type=MESH)

    @pl.when(s > 0)
    def _():
        pl.semaphore_signal(barrier, inc=1, device_id={"layer": s - 1}, device_id_type=MESH)

    @pl.when(s < sections - 1)
    def _():
        pl.semaphore_signal(barrier, inc=1, device_id={"layer": s + 1}, device_id_type=MESH)

    clear(ends)
    clear(last)
    clear(slopes.at[0])
    clear(slopes.at[1])
    clear(states.at[0])
    clear(states.at[1])
    for ref in (z_chain, z_up, z_dn):
        clear(ref)
    z_up[rows(-TOP, TOP + 4)] = jnp.zeros(((TOP + 4) * width, 3 * chans), jnp.bfloat16)
    z_dn[rows(-TOP, TOP + 4)] = jnp.zeros(((TOP + 4) * width, 3 * chans), jnp.bfloat16)
    grad[...] = jnp.zeros(grad.shape, jnp.float32)

    for copy in first[:3]:
        copy.wait()
    rest = [load(kernels_hbm.at[1], kern.at[1], load_sems.at[5])]
    for i in range(2):
        rest.append(load(guess_hbm.at[1, i], image(last, i), load_sems.at[6 + i]))
        rest.append(load(slopes_hbm.at[1, i], image(slopes.at[1], i), load_sems.at[8 + i]))
        for l in range(2):
            rest.append(load(states_hbm.at[l, i], image(states.at[l], i), load_sems.at[10 + 2 * l + i]))

    def spread(z, start, count, slope, values):
        cot = slope.astype(jnp.float32) * values
        size = count * width
        col = lax.broadcasted_iota(jnp.int32, (size, chans), 0) % width
        z[rows(start, count), chans:2 * chans] = cot.astype(jnp.bfloat16)
        ahead = jnp.where(col == width - 1, 0.0, pltpu.roll(cot, size - 1, 0))
        z[rows(start, count), 0:chans] = ahead.astype(jnp.bfloat16)
        behind = jnp.where(col == 0, 0.0, pltpu.roll(cot, 1, 0))
        z[rows(start, count), 2 * chans:3 * chans] = behind.astype(jnp.bfloat16)

    def conv(z, layer, start, count):
        total = None
        for a in range(3):
            for b in range(3):
                piece = z[rows(start + 1 - a, count), b * chans:(b + 1) * chans]
                term = lax.dot_general(
                    piece, kern[layer, 3 * a + b], (((1,), (1,)), ((), ())),
                    preferred_element_type=jnp.float32,
                )
                total = term if total is None else total + term
        return total

    def sends(base, size, hop):
        start = base + 1 - hop
        return (start + size - 1 >= 1) & (start <= end_row)

    def chunk(src, k, base, size):
        where = rows(base + 1 - h, size)
        return pltpu.make_async_remote_copy(
            src_ref=src.at[where],
            dst_ref=recv.at[where],
            send_sem=send_sems.at[k],
            recv_sem=recv_sems.at[k],
            device_id={"layer": s - 1},
            device_id_type=MESH,
        )

    def arrival(k, base, size):
        where = rows(base + 2 - h, size)
        return pltpu.make_async_remote_copy(
            src_ref=recv.at[where],
            dst_ref=recv.at[where],
            send_sem=send_sems.at[k],
            recv_sem=recv_sems.at[k],
            device_id={"layer": s - 1},
            device_id_type=MESH,
        )

    def spread_end(j):
        at = rows(BLK * j, BLK)
        spread(z_chain, BLK * j, BLK, slopes[0, at], ends[at])

    blocks = -(-(end_row + 1) // BLK)
    coarse = (end_row - 1) // BLK
    spread_end(0)

    @pl.loop(0, blocks)
    def _(j):
        @pl.when(j == image_row[1] // BLK - 1)
        def _():
            for copy in first[3:]:
                copy.wait()

        @pl.when(j < blocks - 1)
        def _():
            spread_end(j + 1)

        at = rows(BLK * j, BLK)
        ends[at] = ends[at] + STEP * conv(z_chain, 0, BLK * j, BLK)

        @pl.when(j == 0)
        def _():
            peers = 4 + jnp.where(s > 0, 1, 0) + jnp.where(s < sections - 1, 1, 0)
            pl.semaphore_wait(barrier, peers)

        @pl.when((h == 0) & (s > 0))
        def _():
            for q in range(Q):
                k = Q * j - 1 + q

                @pl.when((k >= 0) & (k < Q * coarse))
                def _():
                    chunk(ends, k, R * k, R).start()

    @pl.when((h == 0) & (s > 0))
    def _():
        chunk(ends, Q * coarse, BLK * coarse, 1).start()

    for copy in rest:
        copy.wait()

    @pl.when(h == 0)
    def _():
        for i in range(2):
            at = rows(image_row[i], height)
            recv[at] = last[at]

    def fine(j, piece):
        start = BLK * (j - 1) + 2 - jnp.maximum(h, 1)

        def gradient(layer, z, at):
            lhs = jnp.concatenate(
                [states[layer, rows(at + a - 1, BLK)].T for a in range(3)], axis=0
            )
            for b in range(3):
                term = jnp.dot(lhs, z[rows(at, BLK), b * chans:(b + 1) * chans],
                               preferred_element_type=jnp.float32)
                for a in range(3):
                    part = term[a * chans:(a + 1) * chans]
                    grad[9 * layer + 3 * a + b] += part.reshape(grad.shape[1:])

        if piece == 0:
            at = rows(start, BLK)
            spread(z_up, start, BLK, slopes[1, at], recv[at])
            at = rows(start - 1, BLK)
            mid[at] = recv[at] + STEP * conv(z_up, 1, start - 1, BLK)
        elif piece == 1:
            at = rows(start - 1, BLK)
            spread(z_dn, start - 1, BLK, slopes[0, at], mid[at])
            at = rows(start - 2, BLK + 1)
            low[at] = mid[at] + STEP * conv(z_dn, 0, start - 2, BLK + 1)
        elif piece == 2:
            gradient(1, z_up, start)
        else:
            gradient(0, z_dn, start - 1)

    def step(k, base, size):
        taken = (h > 0) & sends(base, size, h - 1)

        @pl.when(taken)
        def _():
            arrival(k, base, size).wait_recv()

        @pl.when(taken & (s > 0))
        def _():
            at = rows(base + 2 - h, size)
            spread(z_chain, base + 2 - h, size, slopes[0, at], recv[at] - last[at])

        @pl.when((h > 0) & (s > 0) & sends(base, size, h))
        def _():
            at = rows(base + 1 - h, size)
            send[at] = ((recv[at] - last[at]) + 2 * STEP * conv(z_chain, 0, base + 1 - h, size)) + ends[at]
            chunk(send, k, base, size).start()

    @pl.loop(0, coarse)
    def _(j):
        for q in range(Q):
            step(Q * j + q, BLK * j + R * q, R)

            @pl.when(j > 0)
            def _():
                fine(j, q)

    for i in range(BLK):
        step(Q * coarse + i, BLK * coarse + i, 1)
        if i % 2 == 1:
            fine(coarse, i // 2)

    def remote(src, dst, send_sem, recv_sem, peer):
        return pltpu.make_async_remote_copy(
            src_ref=src, dst_ref=dst, send_sem=send_sem, recv_sem=recv_sem,
            device_id={"dp": peer}, device_id_type=MESH,
        )

    def part(u):
        return slice(PART * u, PART * (u + 1))

    parts = grad.shape[0] // PART
    half = ring // 2

    def core_copy(u):
        return remote(grad.at[part(u), :, :, 1 - core], core_in.at[part(u)],
                      core_sems.at[0, u], core_sems.at[1, u], beside)

    def ring_target(way, away):
        return (depth + away) % ring if way == 0 else (depth + ring - away) % ring

    def carries(way, j, u):
        return u in RING_FIRST or j > 0 or way == u % 2

    def ring_copy(way, j, u):
        target = ring_target(way, half - j)
        if u in CROSS_FIRST:
            src, dst = grad.at[part(u), target, cross, core], ring_in.at[way, j, part(u), 0]
        elif j == 0:
            src, dst = grad.at[part(u), target, way, core], ring_in.at[way, j, part(u), way]
        else:
            src, dst = grad.at[part(u), target, :, core], ring_in.at[way, j, part(u)]
        return remote(src, dst, ring_send.at[way, j, u], ring_recv.at[way, j, u],
                      after if way == 0 else before)

    def add_arrived(way, j, u):
        if not carries(way, j, u):
            return
        ring_copy(way, j, u).wait_recv()
        target = ring_target(way, half - 1 - j)
        if u in CROSS_FIRST:
            grad[part(u), target, cross, core] += ring_in[way, j, part(u), 0]
        elif j == 0:
            grad[part(u), target, way, core] += ring_in[way, j, part(u), way]
        else:
            grad[part(u), target, :, core] += ring_in[way, j, part(u)]

    def ring_round(j, pieces):
        for u in pieces:
            for way in range(2):
                if j > 0:
                    add_arrived(way, j - 1, u)
                if j < half and carries(way, j, u):
                    ring_copy(way, j, u).start()

    def wide_part(u):
        first_tap = PART * (u - CROSS_FIRST[0])
        return slice(first_tap, first_tap + PART)

    def cross_copy(u):
        if u in CROSS_FIRST:
            src, dst = grad.at[part(u), :, 1 - cross, core], wide_in.at[wide_part(u)]
        else:
            src, dst = grad.at[part(u), depth, 1 - cross, core], cross_in.at[part(u)]
        return remote(src, dst, cross_sems.at[0, u], cross_sems.at[1, u], over)

    fine(coarse + 1, 0)
    fine(coarse + 1, 2)
    for u in CROSS_FIRST + RING_FIRST[:1]:
        core_copy(u).start()
    fine(coarse + 1, 1)
    fine(coarse + 1, 3)
    for u in RING_FIRST[1:]:
        core_copy(u).start()
    outs = [load(image(low, i), lower_hbm.at[i], out_sems.at[i]) for i in range(2)]

    for u in CROSS_FIRST + RING_FIRST:
        core_copy(u).wait_recv()
        grad[part(u), :, :, core] += core_in[part(u)]
        if u in CROSS_FIRST:
            cross_copy(u).start()
        else:
            ring_round(0, (u,))
    ring_round(1, RING_FIRST)
    for u in CROSS_FIRST:
        cross_copy(u).wait_recv()
        grad[part(u), :, cross, core] += wide_in[wide_part(u)]
    ring_round(0, CROSS_FIRST)
    for j in range(2, half + 1):
        ring_round(j, RING_FIRST)
        if j == half:
            for u in RING_FIRST:
                cross_copy(u).start()
        ring_round(j - 1, CROSS_FIRST)
    ring_round(half, CROSS_FIRST)
    for u in CROSS_FIRST:
        result[part(u)] = grad[part(u), depth, cross, core] * scale
    for u in RING_FIRST:
        cross_copy(u).wait_recv()
        result[part(u)] = (grad[part(u), depth, cross, core] + cross_in[part(u)]) * scale
    outs.append(load(result, grad_hbm, out_sems.at[2]))

    for u in range(parts):
        core_copy(u).wait_send()
        cross_copy(u).wait_send()
        for j in range(half):
            for way in range(2):
                if carries(way, j, u):
                    ring_copy(way, j, u).wait_send()

    @pl.loop(0, Q * coarse)
    def _(k):
        @pl.when((s > 0) & sends(R * k, R, h))
        def _():
            chunk(send, k, R * k, R).wait_send()

    for i in range(BLK):
        @pl.when((s > 0) & sends(BLK * coarse + i, 1, h))
        def _():
            chunk(send, Q * coarse + i, BLK * coarse + i, 1).wait_send()

    for copy in outs:
        copy.wait()


def deliver(lower_in, grads_in, lower_out, grads_out, sems):
    copies = [pltpu.make_async_copy(grads_in, grads_out, sems.at[0])]
    size = lower_in.shape[1] // 4
    for i in range(lower_in.shape[0]):
        for j in range(4):
            where = pl.ds(size * j, size)
            copies.append(pltpu.make_async_copy(
                lower_in.at[i, where], lower_out.at[i, where], sems.at[1 + 4 * i + j]))
    for copy in copies:
        copy.start()
    for copy in copies:
        copy.wait()


def on_device(states, slopes, kernels, guess):
    layers, images, height, width, chans = states.shape
    sections = lax.axis_size("layer")
    replicas = lax.axis_size("dp")
    scale = STEP / (images * replicas)
    pix = height * width
    flat = lambda array: array.reshape(layers, images, pix, chans)
    steps = Q * (2 * height // BLK) + BLK
    size = ROWS * width
    any_space = pl.BlockSpec(memory_space=pl.ANY)
    f32, bf16 = jnp.float32, jnp.bfloat16
    ring = replicas // 4
    share = chans // replicas
    lower, grads = pl.pallas_call(
        functools.partial(chain_kernel, sections, scale, height, width, chans),
        out_shape=(
            jax.ShapeDtypeStruct((images, pix, chans), f32),
            jax.ShapeDtypeStruct((layers * 9, chans // replicas, chans), f32),
        ),
        in_specs=[any_space] * 4,
        out_specs=(any_space, any_space),
        scratch_shapes=[
            pltpu.VMEM((layers, size, chans), bf16),
            pltpu.VMEM((layers, size, chans), bf16),
            pltpu.VMEM((layers, 9, chans, chans), bf16),
            pltpu.VMEM((size, chans), f32),
            pltpu.VMEM((size, chans), f32),
            pltpu.VMEM((size, chans), f32),
            pltpu.VMEM((size, chans), f32),
            pltpu.VMEM((size, chans), f32),
            pltpu.VMEM((size, chans), f32),
            pltpu.VMEM((size, 3 * chans), bf16),
            pltpu.VMEM((size, 3 * chans), bf16),
            pltpu.VMEM((size, 3 * chans), bf16),
            pltpu.VMEM((layers * 9, ring, 2, 2, share, chans), f32),
            pltpu.VMEM((layers * 9, ring, 2, share, chans), f32),
            pltpu.VMEM((2, ring // 2, layers * 9, 2, share, chans), f32),
            pltpu.VMEM((layers * 9, share, chans), f32),
            pltpu.VMEM((len(CROSS_FIRST) * PART, ring, share, chans), f32),
            pltpu.VMEM((layers * 9, share, chans), f32),
            pltpu.SemaphoreType.DMA((14,)),
            pltpu.SemaphoreType.DMA((steps,)),
            pltpu.SemaphoreType.DMA((steps,)),
            pltpu.SemaphoreType.DMA((3,)),
            pltpu.SemaphoreType.DMA((2, layers * 9 // PART)),
            pltpu.SemaphoreType.DMA((2, ring // 2, layers * 9 // PART)),
            pltpu.SemaphoreType.DMA((2, ring // 2, layers * 9 // PART)),
            pltpu.SemaphoreType.DMA((2, layers * 9 // PART)),
        ],
        compiler_params=pltpu.CompilerParams(
            collective_id=0, has_side_effects=True, vmem_limit_bytes=60 * 1024 * 1024
        ),
    )(flat(states), flat(slopes), kernels, flat(guess))
    lower, grads = pl.pallas_call(
        deliver,
        out_shape=(
            jax.ShapeDtypeStruct(lower.shape, f32),
            jax.ShapeDtypeStruct(grads.shape, f32),
        ),
        in_specs=[any_space] * 2,
        out_specs=(any_space, any_space),
        scratch_shapes=[pltpu.SemaphoreType.DMA((1 + 4 * images,))],
    )(lower, grads)
    return (
        lower.reshape(1, images, height, width, chans),
        grads.reshape(layers, 9, share, chans),
    )


def solution(mesh):
    return jax.shard_map(
        on_device,
        mesh=mesh,
        in_specs=(
            P("layer", "dp", None, None, None),
            P("layer", "dp", None, None, None),
            P("layer", None, None, None),
            P("layer", "dp", None, None, None),
        ),
        out_specs=(P("layer", "dp", None, None, None), P("layer", None, "dp", None)),
        check_vma=False,
    )
```

```python
import functools

import jax
import jax.numpy as jnp
from jax import lax
from jax.experimental import pallas as pl
from jax.experimental.pallas import tpu as pltpu
from jax.sharding import PartitionSpec as P

MESH = pl.DeviceIdType.MESH
STEP = 0.5
TOP = 8
ROWS = 88
R = 2
Q = 4
BLK = R * Q
PART = 3
RING_FIRST = (3, 0, 1, 2)
CROSS_FIRST = (4, 5)


def chain_kernel(
    sections, scale, height, width, chans,
    states_hbm, slopes_hbm, kernels_hbm, guess_hbm,
    lower_hbm, grad_hbm,
    states, slopes, kern, kern_t, last, ends, recv, send, mid, low, z_chain, z_up, z_dn, grad,
    core_in, ring_in, cross_in, wide_in, result,
    load_sems, send_sems, recv_sems, out_sems,
    core_sems, ring_send, ring_recv, cross_sems, wide_sems,
):
    s = lax.axis_index("layer")
    h = sections - 1 - s
    pix = height * width
    image_row = (1, height + 2)
    end_row = 2 * height + 1

    def rows(start, count):
        return pl.ds(pl.multiple_of((start + TOP) * width, width), count * width)

    def image(ref, i):
        return ref.at[rows(image_row[i], height)]

    def load(src, dst, sem):
        copy = pltpu.make_async_copy(src, dst, sem)
        copy.start()
        return copy

    pads = ((-TOP, TOP + 1), (height + 1, 1), (end_row + 1, ROWS - TOP - end_row - 1))

    def clear(ref):
        for start, count in pads:
            part = ref.at[rows(start, count)]
            part[...] = jnp.zeros(part.shape, part.dtype)

    first = [load(kernels_hbm.at[0], kern.at[0], load_sems.at[0])]
    for i in range(2):
        first.append(load(guess_hbm.at[0, i], image(ends, i), load_sems.at[1 + i]))
        first.append(load(slopes_hbm.at[0, i], image(slopes.at[0], i), load_sems.at[3 + i]))
    place = lax.axis_index("dp")
    ring = lax.axis_size("dp") // 4
    depth = place // 4
    cross = (place // 2) % 2
    core = place % 2
    beside = place + 1 - 2 * core
    over = place + 2 - 4 * cross
    after = ((depth + 1) % ring) * 4 + place % 4
    before = ((depth + ring - 1) % ring) * 4 + place % 4

    clear(recv)
    barrier = pltpu.get_barrier_semaphore()
    for peer in (beside, over, after, before):
        pl.semaphore_signal(barrier, inc=1, device_id={"dp": peer}, device_id_type=MESH)

    @pl.when(s > 0)
    def _():
        pl.semaphore_signal(barrier, inc=1, device_id={"layer": s - 1}, device_id_type=MESH)

    @pl.when(s < sections - 1)
    def _():
        pl.semaphore_signal(barrier, inc=1, device_id={"layer": s + 1}, device_id_type=MESH)

    clear(ends)
    clear(last)
    clear(slopes.at[0])
    clear(slopes.at[1])
    clear(states.at[0])
    clear(states.at[1])
    for ref in (z_chain, z_up, z_dn):
        clear(ref)
    z_up[rows(-TOP, TOP + 4)] = jnp.zeros(((TOP + 4) * width, 3 * chans), jnp.bfloat16)
    z_dn[rows(-TOP, TOP + 4)] = jnp.zeros(((TOP + 4) * width, 3 * chans), jnp.bfloat16)
    grad[...] = jnp.zeros(grad.shape, jnp.float32)

    for copy in first[:3]:
        copy.wait()
    rest = [load(kernels_hbm.at[1], kern.at[1], load_sems.at[5])]
    for i in range(2):
        rest.append(load(guess_hbm.at[1, i], image(last, i), load_sems.at[6 + i]))
        rest.append(load(slopes_hbm.at[1, i], image(slopes.at[1], i), load_sems.at[8 + i]))
        for l in range(2):
            rest.append(load(states_hbm.at[l, i], image(states.at[l], i), load_sems.at[10 + 2 * l + i]))

    def spread(z, start, count, slope, values):
        cot = slope.astype(jnp.float32) * values
        size = count * width
        col = lax.broadcasted_iota(jnp.int32, (size, chans), 0) % width
        z[rows(start, count), chans:2 * chans] = cot.astype(jnp.bfloat16)
        ahead = jnp.where(col == width - 1, 0.0, pltpu.roll(cot, size - 1, 0))
        z[rows(start, count), 0:chans] = ahead.astype(jnp.bfloat16)
        behind = jnp.where(col == 0, 0.0, pltpu.roll(cot, 1, 0))
        z[rows(start, count), 2 * chans:3 * chans] = behind.astype(jnp.bfloat16)

    def conv(z, layer, start, count):
        total = None
        for a in range(3):
            term = jnp.dot(z[rows(start + 1 - a, count), :], kern_t[layer, a],
                           preferred_element_type=jnp.float32)
            total = term if total is None else total + term
        return total

    def turn(layer):
        for a in range(3):
            for b in range(3):
                kern_t[layer, a, b * chans:(b + 1) * chans] = kern[layer, 3 * a + b].T

    def sends(base, size, hop):
        start = base + 1 - hop
        return (start + size - 1 >= 1) & (start <= end_row)

    def chunk(src, k, start, size):
        where = rows(start, size)
        return pltpu.make_async_remote_copy(
            src_ref=src.at[where],
            dst_ref=recv.at[where],
            send_sem=send_sems.at[k],
            recv_sem=recv_sems.at[k],
            device_id={"layer": s - 1},
            device_id_type=MESH,
        )

    def each_chunk(start, size, act):
        if size == 1:
            act(start, 1)
            return
        skip_first = (start == 0) | (start == height + 1)
        skip_last = start == height

        @pl.when(jnp.logical_not(skip_first | skip_last))
        def _():
            act(start, size)

        @pl.when(skip_first)
        def _():
            act(start + 1, size - 1)

        @pl.when(skip_last)
        def _():
            act(start, size - 1)

    def start_chunk(src, k, base, size):
        each_chunk(base + 1 - h, size, lambda at, count: chunk(src, k, at, count).start())

    def sent_chunk(k, base, size):
        each_chunk(base + 1 - h, size, lambda at, count: chunk(send, k, at, count).wait_send())

    def arrived_chunk(k, base, size):
        each_chunk(base + 2 - h, size, lambda at, count: chunk(recv, k, at, count).wait_recv())

    def spread_end(j):
        at = rows(BLK * j, BLK)
        spread(z_chain, BLK * j, BLK, slopes[0, at], ends[at])

    blocks = -(-(end_row + 1) // BLK)
    coarse = (end_row - 1) // BLK
    turn(0)
    spread_end(0)

    @pl.loop(0, blocks)
    def _(j):
        @pl.when(j == image_row[1] // BLK - 1)
        def _():
            for copy in first[3:]:
                copy.wait()

        @pl.when(j < blocks - 1)
        def _():
            spread_end(j + 1)

        at = rows(BLK * j, BLK)
        ends[at] = ends[at] + STEP * conv(z_chain, 0, BLK * j, BLK)

        @pl.when(j == 0)
        def _():
            peers = 4 + jnp.where(s > 0, 1, 0) + jnp.where(s < sections - 1, 1, 0)
            pl.semaphore_wait(barrier, peers)

        @pl.when((h == 0) & (s > 0))
        def _():
            for q in range(Q):
                k = Q * j - 1 + q

                @pl.when((k >= 0) & (k < Q * coarse))
                def _():
                    start_chunk(ends, k, R * k, R)

    @pl.when((h == 0) & (s > 0))
    def _():
        start_chunk(ends, Q * coarse, BLK * coarse, 1)

    for copy in rest:
        copy.wait()
    turn(1)

    @pl.when(h == 0)
    def _():
        for i in range(2):
            at = rows(image_row[i], height)
            recv[at] = last[at]

    def fine(j, piece):
        start = BLK * (j - 1) + 2 - jnp.maximum(h, 1)

        def gradient(layer, z, at):
            lhs = jnp.concatenate(
                [states[layer, rows(at + a - 1, BLK)].T for a in range(3)], axis=0
            )
            for b in range(3):
                term = jnp.dot(lhs, z[rows(at, BLK), b * chans:(b + 1) * chans],
                               preferred_element_type=jnp.float32)
                for a in range(3):
                    part = term[a * chans:(a + 1) * chans]
                    part = part.reshape(grad.shape[2:4] + (2,) + grad.shape[4:])
                    for c in range(2):
                        grad[c, 9 * layer + 3 * a + b] += part[:, :, c]

        if piece == 0:
            at = rows(start, BLK)
            spread(z_up, start, BLK, slopes[1, at], recv[at])
            at = rows(start - 1, BLK)
            mid[at] = recv[at] + STEP * conv(z_up, 1, start - 1, BLK)
        elif piece == 1:
            at = rows(start - 1, BLK)
            spread(z_dn, start - 1, BLK, slopes[0, at], mid[at])
            at = rows(start - 2, BLK + 1)
            low[at] = mid[at] + STEP * conv(z_dn, 0, start - 2, BLK + 1)
        elif piece == 2:
            gradient(1, z_up, start)
        else:
            gradient(0, z_dn, start - 1)

    def step(k, base, size):
        taken = (h > 0) & sends(base, size, h - 1)

        @pl.when(taken)
        def _():
            arrived_chunk(k, base, size)

        @pl.when(taken & (s > 0))
        def _():
            at = rows(base + 2 - h, size)
            spread(z_chain, base + 2 - h, size, slopes[0, at], recv[at] - last[at])

        @pl.when((h > 0) & (s > 0) & sends(base, size, h))
        def _():
            at = rows(base + 1 - h, size)
            send[at] = ((recv[at] - last[at]) + 2 * STEP * conv(z_chain, 0, base + 1 - h, size)) + ends[at]
            start_chunk(send, k, base, size)

    @pl.loop(0, coarse)
    def _(j):
        for q in range(Q):
            step(Q * j + q, BLK * j + R * q, R)

            @pl.when(j > 0)
            def _():
                fine(j, q)

    for i in range(BLK):
        step(Q * coarse + i, BLK * coarse + i, 1)
        if i % 2 == 1:
            fine(coarse, i // 2)

    def remote(src, dst, send_sem, recv_sem, peer):
        return pltpu.make_async_remote_copy(
            src_ref=src, dst_ref=dst, send_sem=send_sem, recv_sem=recv_sem,
            device_id={"dp": peer}, device_id_type=MESH,
        )

    def part(u):
        return slice(PART * u, PART * (u + 1))

    parts = grad.shape[1] // PART
    half = ring // 2
    slices = [half] + [sign * away for away in range(half - 1, 0, -1) for sign in (1, -1)] + [0]

    def core_copy(u):
        return remote(grad.at[1 - core, part(u)], core_in.at[part(u)],
                      core_sems.at[0, u], core_sems.at[1, u], beside)

    def ring_target(way, away):
        return (depth + away) % ring if way == 0 else (depth + ring - away) % ring

    def carries(way, j, u):
        return u in RING_FIRST or j > 0 or way == u % 2

    def ring_copy(way, j, u):
        target = ring_target(way, half - j)
        if u in CROSS_FIRST:
            src, dst = grad.at[core, part(u), target, cross], ring_in.at[way, j, part(u), 0]
        elif j == 0:
            src, dst = grad.at[core, part(u), target, way], ring_in.at[way, j, part(u), way]
        else:
            src, dst = grad.at[core, part(u), target], ring_in.at[way, j, part(u)]
        return remote(src, dst, ring_send.at[way, j, u], ring_recv.at[way, j, u],
                      after if way == 0 else before)

    def add_arrived(way, j, u):
        if not carries(way, j, u):
            return
        ring_copy(way, j, u).wait_recv()
        target = ring_target(way, half - 1 - j)
        if u in CROSS_FIRST:
            grad[core, part(u), target, cross] += ring_in[way, j, part(u), 0]
        elif j == 0:
            grad[core, part(u), target, way] += ring_in[way, j, part(u), way]
        else:
            grad[core, part(u), target] += ring_in[way, j, part(u)]

    def ring_round(j, pieces):
        for u in pieces:
            if u in CROSS_FIRST:
                for n, away in enumerate(slices):
                    if abs(away) == half - j:
                        add_wide(u, n)
            for way in range(2):
                if j > 0:
                    add_arrived(way, j - 1, u)
                if j < half and carries(way, j, u):
                    ring_copy(way, j, u).start()

    def wide_part(u):
        first_tap = PART * (u - CROSS_FIRST[0])
        return slice(first_tap, first_tap + PART)

    def cross_copy(u):
        return remote(grad.at[core, part(u), depth, 1 - cross], cross_in.at[part(u)],
                      cross_sems.at[0, u], cross_sems.at[1, u], over)

    def wide_copy(u, n):
        target = (depth + slices[n]) % ring
        return remote(grad.at[core, part(u), target, 1 - cross], wide_in.at[wide_part(u), n],
                      wide_sems.at[0, u - CROSS_FIRST[0], n],
                      wide_sems.at[1, u - CROSS_FIRST[0], n], over)

    def add_wide(u, n):
        wide_copy(u, n).wait_recv()
        target = (depth + slices[n]) % ring
        grad[core, part(u), target, cross] += wide_in[wide_part(u), n]

    fine(coarse + 1, 0)
    fine(coarse + 1, 2)
    early = RING_FIRST[:1] + CROSS_FIRST
    for u in early:
        core_copy(u).start()
    fine(coarse + 1, 1)
    fine(coarse + 1, 3)
    for u in RING_FIRST[1:]:
        core_copy(u).start()
    outs = [load(image(low, i), lower_hbm.at[i], out_sems.at[i]) for i in range(2)]

    for u in early + RING_FIRST[1:]:
        core_copy(u).wait_recv()
        grad[core, part(u)] += core_in[part(u)]
        if u in CROSS_FIRST:
            for n in range(ring):
                wide_copy(u, n).start()
        else:
            ring_round(0, (u,))
    ring_round(1, RING_FIRST)
    ring_round(0, CROSS_FIRST)
    for j in range(2, half + 1):
        ring_round(j, RING_FIRST)
        if j == half:
            for u in RING_FIRST:
                cross_copy(u).start()
        ring_round(j - 1, CROSS_FIRST)
    for u in range(parts):
        core_copy(u).wait_send()
        if u in CROSS_FIRST:
            for n in range(ring):
                wide_copy(u, n).wait_send()
        for j in range(half):
            for way in range(2):
                if carries(way, j, u) and (u in RING_FIRST or j < half - 1):
                    ring_copy(way, j, u).wait_send()
    for copy in outs:
        copy.wait()

    @pl.loop(0, Q * coarse)
    def _(k):
        @pl.when((s > 0) & sends(R * k, R, h))
        def _():
            sent_chunk(k, R * k, R)

    for i in range(BLK):
        @pl.when((s > 0) & sends(BLK * coarse + i, 1, h))
        def _():
            sent_chunk(Q * coarse + i, BLK * coarse + i, 1)

    ring_round(half, CROSS_FIRST)
    for u in CROSS_FIRST:
        result[part(u)] = grad[core, part(u), depth, cross] * scale
    for u in RING_FIRST:
        cross_copy(u).wait_recv()
        result[part(u)] = (grad[core, part(u), depth, cross] + cross_in[part(u)]) * scale
    outs = [load(result, grad_hbm, out_sems.at[2])]

    for u in range(parts):
        if u in CROSS_FIRST:
            for way in range(2):
                ring_copy(way, half - 1, u).wait_send()
        else:
            cross_copy(u).wait_send()
    for copy in outs:
        copy.wait()


def deliver(lower_in, grads_in, lower_out, grads_out, lower_held, grads_held, sems):
    pieces = [(grads_in, grads_held, grads_out)]
    size = lower_in.shape[1] // 2
    for i in range(lower_in.shape[0]):
        for j in range(2):
            where = (i, pl.ds(size * j, size))
            pieces.append((lower_in.at[where], lower_held.at[where], lower_out.at[where]))
    ins = [pltpu.make_async_copy(p[0], p[1], sems.at[0, n]) for n, p in enumerate(pieces)]
    outs = [pltpu.make_async_copy(p[1], p[2], sems.at[1, n]) for n, p in enumerate(pieces)]
    for copy in ins:
        copy.start()
    for arrived, copy in zip(ins, outs):
        arrived.wait()
        copy.start()
    for copy in outs:
        copy.wait()


def on_device(states, slopes, kernels, guess):
    layers, images, height, width, chans = states.shape
    sections = lax.axis_size("layer")
    replicas = lax.axis_size("dp")
    scale = STEP / (images * replicas)
    pix = height * width
    flat = lambda array: array.reshape(layers, images, pix, chans)
    steps = Q * (2 * height // BLK) + BLK
    size = ROWS * width
    any_space = pl.BlockSpec(memory_space=pl.ANY)
    f32, bf16 = jnp.float32, jnp.bfloat16
    ring = replicas // 4
    share = chans // replicas
    lower, grads = pl.pallas_call(
        functools.partial(chain_kernel, sections, scale, height, width, chans),
        out_shape=(
            jax.ShapeDtypeStruct((images, pix, chans), f32),
            jax.ShapeDtypeStruct((layers * 9, chans // replicas, chans), f32),
        ),
        in_specs=[any_space] * 4,
        out_specs=(any_space, any_space),
        scratch_shapes=[
            pltpu.VMEM((layers, size, chans), bf16),
            pltpu.VMEM((layers, size, chans), bf16),
            pltpu.VMEM((layers, 9, chans, chans), bf16),
            pltpu.VMEM((layers, 3, 3 * chans, chans), bf16),
            pltpu.VMEM((size, chans), f32),
            pltpu.VMEM((size, chans), f32),
            pltpu.VMEM((size, chans), f32),
            pltpu.VMEM((size, chans), f32),
            pltpu.VMEM((size, chans), f32),
            pltpu.VMEM((size, chans), f32),
            pltpu.VMEM((size, 3 * chans), bf16),
            pltpu.VMEM((size, 3 * chans), bf16),
            pltpu.VMEM((size, 3 * chans), bf16),
            pltpu.VMEM((2, layers * 9, ring, 2, share, chans), f32),
            pltpu.VMEM((layers * 9, ring, 2, share, chans), f32),
            pltpu.VMEM((2, ring // 2, layers * 9, 2, share, chans), f32),
            pltpu.VMEM((layers * 9, share, chans), f32),
            pltpu.VMEM((len(CROSS_FIRST) * PART, ring, share, chans), f32),
            pltpu.VMEM((layers * 9, share, chans), f32),
            pltpu.SemaphoreType.DMA((14,)),
            pltpu.SemaphoreType.DMA((steps,)),
            pltpu.SemaphoreType.DMA((steps,)),
            pltpu.SemaphoreType.DMA((3,)),
            pltpu.SemaphoreType.DMA((2, layers * 9 // PART)),
            pltpu.SemaphoreType.DMA((2, ring // 2, layers * 9 // PART)),
            pltpu.SemaphoreType.DMA((2, ring // 2, layers * 9 // PART)),
            pltpu.SemaphoreType.DMA((2, layers * 9 // PART)),
            pltpu.SemaphoreType.DMA((2, len(CROSS_FIRST), ring)),
        ],
        compiler_params=pltpu.CompilerParams(
            collective_id=0, has_side_effects=True, vmem_limit_bytes=60 * 1024 * 1024
        ),
    )(flat(states), flat(slopes), kernels, flat(guess))
    lower, grads = pl.pallas_call(
        deliver,
        out_shape=(
            jax.ShapeDtypeStruct(lower.shape, f32),
            jax.ShapeDtypeStruct(grads.shape, f32),
        ),
        in_specs=[any_space] * 2,
        out_specs=(any_space, any_space),
        scratch_shapes=[
            pltpu.VMEM(lower.shape, f32),
            pltpu.VMEM(grads.shape, f32),
            pltpu.SemaphoreType.DMA((2, 1 + 2 * images)),
        ],
    )(lower, grads)
    return (
        lower.reshape(1, images, height, width, chans),
        grads.reshape(layers, 9, share, chans),
    )


def solution(mesh):
    return jax.shard_map(
        on_device,
        mesh=mesh,
        in_specs=(
            P("layer", "dp", None, None, None),
            P("layer", "dp", None, None, None),
            P("layer", None, None, None),
            P("layer", "dp", None, None, None),
        ),
        out_specs=(P("layer", "dp", None, None, None), P("layer", None, "dp", None)),
        check_vma=False,
    )
```

```python
import functools

import jax
import jax.numpy as jnp
from jax import lax
from jax.experimental import pallas as pl
from jax.experimental.pallas import tpu as pltpu
from jax.sharding import PartitionSpec as P

MESH = pl.DeviceIdType.MESH
STEP = 0.5
TOP = 8
ROWS = 88
R = 2
Q = 4
BLK = R * Q
PART = 3
RING_FIRST = (3, 0, 1, 2)
CROSS_FIRST = (4, 5)


def chain_kernel(
    sections, scale, height, width, chans,
    states_hbm, slopes_hbm, kernels_hbm, guess_hbm,
    lower_hbm, grad_hbm,
    states, slopes, kern, kern_t, last, ends, recv, send, mid, low, z_chain, z_up, z_dn, grad,
    core_in, ring_in, cross_in, wide_in, result,
    load_sems, send_sems, recv_sems, out_sems,
    core_sems, ring_send, ring_recv, cross_sems, wide_sems,
):
    s = lax.axis_index("layer")
    h = sections - 1 - s
    pix = height * width
    image_row = (1, height + 2)
    end_row = 2 * height + 1

    def rows(start, count):
        return pl.ds(pl.multiple_of((start + TOP) * width, width), count * width)

    def image(ref, i):
        return ref.at[rows(image_row[i], height)]

    def load(src, dst, sem):
        copy = pltpu.make_async_copy(src, dst, sem)
        copy.start()
        return copy

    pads = ((-TOP, TOP + 1), (height + 1, 1), (end_row + 1, ROWS - TOP - end_row - 1))

    def clear(ref):
        for start, count in pads:
            part = ref.at[rows(start, count)]
            part[...] = jnp.zeros(part.shape, part.dtype)

    first = [load(kernels_hbm.at[0], kern.at[0], load_sems.at[0])]
    for i in range(2):
        first.append(load(guess_hbm.at[0, i], image(ends, i), load_sems.at[1 + i]))
        first.append(load(slopes_hbm.at[0, i], image(slopes.at[0], i), load_sems.at[3 + i]))
    place = lax.axis_index("dp")
    ring = lax.axis_size("dp") // 4
    depth = place // 4
    cross = (place // 2) % 2
    core = place % 2
    beside = place + 1 - 2 * core
    over = place + 2 - 4 * cross
    after = ((depth + 1) % ring) * 4 + place % 4
    before = ((depth + ring - 1) % ring) * 4 + place % 4

    clear(recv)
    barrier = pltpu.get_barrier_semaphore()
    for peer in (beside, over, after, before):
        pl.semaphore_signal(barrier, inc=1, device_id={"dp": peer}, device_id_type=MESH)

    @pl.when(s > 0)
    def _():
        pl.semaphore_signal(barrier, inc=1, device_id={"layer": s - 1}, device_id_type=MESH)

    @pl.when(s < sections - 1)
    def _():
        pl.semaphore_signal(barrier, inc=1, device_id={"layer": s + 1}, device_id_type=MESH)

    clear(ends)
    clear(last)
    clear(slopes.at[0])
    clear(slopes.at[1])
    clear(states.at[0])
    clear(states.at[1])
    for ref in (z_chain, z_up, z_dn):
        clear(ref)
    z_up[rows(-TOP, TOP + 4)] = jnp.zeros(((TOP + 4) * width, 3 * chans), jnp.bfloat16)
    z_dn[rows(-TOP, TOP + 4)] = jnp.zeros(((TOP + 4) * width, 3 * chans), jnp.bfloat16)
    grad[...] = jnp.zeros(grad.shape, jnp.float32)

    for copy in first[:3]:
        copy.wait()
    rest = [load(kernels_hbm.at[1], kern.at[1], load_sems.at[5])]
    for i in range(2):
        rest.append(load(guess_hbm.at[1, i], image(last, i), load_sems.at[6 + i]))
        rest.append(load(slopes_hbm.at[1, i], image(slopes.at[1], i), load_sems.at[8 + i]))
        for l in range(2):
            rest.append(load(states_hbm.at[l, i], image(states.at[l], i), load_sems.at[10 + 2 * l + i]))

    def spread(z, start, count, slope, values):
        cot = slope.astype(jnp.float32) * values
        size = count * width
        col = lax.broadcasted_iota(jnp.int32, (size, chans), 0) % width
        z[rows(start, count), chans:2 * chans] = cot.astype(jnp.bfloat16)
        ahead = jnp.where(col == width - 1, 0.0, pltpu.roll(cot, size - 1, 0))
        z[rows(start, count), 0:chans] = ahead.astype(jnp.bfloat16)
        behind = jnp.where(col == 0, 0.0, pltpu.roll(cot, 1, 0))
        z[rows(start, count), 2 * chans:3 * chans] = behind.astype(jnp.bfloat16)

    def conv(z, layer, start, count):
        total = None
        for a in range(3):
            term = jnp.dot(z[rows(start + 1 - a, count), :], kern_t[layer, a],
                           preferred_element_type=jnp.float32)
            total = term if total is None else total + term
        return total

    def turn(layer):
        for a in range(3):
            for b in range(3):
                kern_t[layer, a, b * chans:(b + 1) * chans] = kern[layer, 3 * a + b].T

    def sends(base, size, hop):
        start = base + 1 - hop
        return (start + size - 1 >= 1) & (start <= end_row)

    def chunk(src, k, start, size):
        where = rows(start, size)
        return pltpu.make_async_remote_copy(
            src_ref=src.at[where],
            dst_ref=recv.at[where],
            send_sem=send_sems.at[k],
            recv_sem=recv_sems.at[k],
            device_id={"layer": s - 1},
            device_id_type=MESH,
        )

    def each_chunk(start, size, act):
        if size == 1:
            act(start, 1)
            return
        skip_first = (start == 0) | (start == height + 1)
        skip_last = start == height

        @pl.when(jnp.logical_not(skip_first | skip_last))
        def _():
            act(start, size)

        @pl.when(skip_first)
        def _():
            act(start + 1, size - 1)

        @pl.when(skip_last)
        def _():
            act(start, size - 1)

    def start_chunk(src, k, base, size):
        each_chunk(base + 1 - h, size, lambda at, count: chunk(src, k, at, count).start())

    def sent_chunk(k, base, size):
        each_chunk(base + 1 - h, size, lambda at, count: chunk(send, k, at, count).wait_send())

    def arrived_chunk(k, base, size):
        each_chunk(base + 2 - h, size, lambda at, count: chunk(recv, k, at, count).wait_recv())

    def spread_end(j):
        at = rows(BLK * j, BLK)
        spread(z_chain, BLK * j, BLK, slopes[0, at], ends[at])

    blocks = -(-(end_row + 1) // BLK)
    coarse = (end_row - 1) // BLK
    turn(0)
    spread_end(0)

    @pl.loop(0, blocks)
    def _(j):
        @pl.when(j == image_row[1] // BLK - 1)
        def _():
            for copy in first[3:]:
                copy.wait()

        @pl.when(j < blocks - 1)
        def _():
            spread_end(j + 1)

        at = rows(BLK * j, BLK)
        ends[at] = ends[at] + STEP * conv(z_chain, 0, BLK * j, BLK)

        @pl.when(j == 0)
        def _():
            peers = 4 + jnp.where(s > 0, 1, 0) + jnp.where(s < sections - 1, 1, 0)
            pl.semaphore_wait(barrier, peers)

        @pl.when((h == 0) & (s > 0))
        def _():
            for q in range(Q):
                k = Q * j - 1 + q

                @pl.when((k >= 0) & (k < Q * coarse))
                def _():
                    start_chunk(ends, k, R * k, R)

    @pl.when((h == 0) & (s > 0))
    def _():
        start_chunk(ends, Q * coarse, BLK * coarse, 1)

    for copy in rest:
        copy.wait()
    turn(1)

    @pl.when(h == 0)
    def _():
        for i in range(2):
            at = rows(image_row[i], height)
            recv[at] = last[at]

    def fine(j, piece):
        start = BLK * (j - 1) + 2 - jnp.maximum(h, 1)

        def gradient(layer, z, at):
            lhs = jnp.concatenate(
                [states[layer, rows(at + a - 1, BLK)].T for a in range(3)], axis=0
            )
            for b in range(3):
                term = jnp.dot(lhs, z[rows(at, BLK), b * chans:(b + 1) * chans],
                               preferred_element_type=jnp.float32)
                for a in range(3):
                    part = term[a * chans:(a + 1) * chans]
                    part = part.reshape(grad.shape[2:4] + (2,) + grad.shape[4:])
                    for c in range(2):
                        grad[c, 9 * layer + 3 * a + b] += part[:, :, c]

        if piece == 0:
            at = rows(start, BLK)
            spread(z_up, start, BLK, slopes[1, at], recv[at])
            at = rows(start - 1, BLK)
            mid[at] = recv[at] + STEP * conv(z_up, 1, start - 1, BLK)
        elif piece == 1:
            at = rows(start - 1, BLK)
            spread(z_dn, start - 1, BLK, slopes[0, at], mid[at])
            at = rows(start - 2, BLK + 1)
            low[at] = mid[at] + STEP * conv(z_dn, 0, start - 2, BLK + 1)
        elif piece == 2:
            gradient(1, z_up, start)
        else:
            gradient(0, z_dn, start - 1)

    def step(k, base, size):
        taken = (h > 0) & sends(base, size, h - 1)

        @pl.when(taken)
        def _():
            arrived_chunk(k, base, size)

        @pl.when(taken & (s > 0))
        def _():
            at = rows(base + 2 - h, size)
            spread(z_chain, base + 2 - h, size, slopes[0, at], recv[at] - last[at])

        @pl.when((h > 0) & (s > 0) & sends(base, size, h))
        def _():
            at = rows(base + 1 - h, size)
            send[at] = ((recv[at] - last[at]) + 2 * STEP * conv(z_chain, 0, base + 1 - h, size)) + ends[at]
            start_chunk(send, k, base, size)

    @pl.loop(0, coarse)
    def _(j):
        for q in range(Q):
            step(Q * j + q, BLK * j + R * q, R)

            @pl.when(j > 0)
            def _():
                fine(j, q)

    for i in range(BLK):
        step(Q * coarse + i, BLK * coarse + i, 1)
        if i % 2 == 1:
            fine(coarse, i // 2)

    def remote(src, dst, send_sem, recv_sem, peer):
        return pltpu.make_async_remote_copy(
            src_ref=src, dst_ref=dst, send_sem=send_sem, recv_sem=recv_sem,
            device_id={"dp": peer}, device_id_type=MESH,
        )

    def part(u):
        return slice(PART * u, PART * (u + 1))

    parts = grad.shape[1] // PART
    half = ring // 2
    slices = [half] + [sign * away for away in range(half - 1, 0, -1) for sign in (1, -1)] + [0]

    def core_copy(u):
        return remote(grad.at[1 - core, part(u)], core_in.at[part(u)],
                      core_sems.at[0, u], core_sems.at[1, u], beside)

    def ring_target(way, away):
        return (depth + away) % ring if way == 0 else (depth + ring - away) % ring

    def carries(way, j, u):
        return u in RING_FIRST or j > 0 or way == u % 2

    def ring_copy(way, j, u):
        target = ring_target(way, half - j)
        if u in CROSS_FIRST:
            src, dst = grad.at[core, part(u), target, cross], ring_in.at[way, j, part(u), 0]
        elif j == 0:
            src, dst = grad.at[core, part(u), target, way], ring_in.at[way, j, part(u), way]
        else:
            src, dst = grad.at[core, part(u), target], ring_in.at[way, j, part(u)]
        return remote(src, dst, ring_send.at[way, j, u], ring_recv.at[way, j, u],
                      after if way == 0 else before)

    def add_arrived(way, j, u):
        if not carries(way, j, u):
            return
        ring_copy(way, j, u).wait_recv()
        target = ring_target(way, half - 1 - j)
        if u in CROSS_FIRST:
            grad[core, part(u), target, cross] += ring_in[way, j, part(u), 0]
        elif j == 0:
            grad[core, part(u), target, way] += ring_in[way, j, part(u), way]
        else:
            grad[core, part(u), target] += ring_in[way, j, part(u)]

    def ring_round(j, pieces):
        for u in pieces:
            if u in CROSS_FIRST:
                for n, away in enumerate(slices):
                    if abs(away) == half - j:
                        add_wide(u, n)
            for way in range(2):
                if j > 0:
                    add_arrived(way, j - 1, u)
                if j < half and carries(way, j, u):
                    ring_copy(way, j, u).start()

    def wide_part(u):
        first_tap = PART * (u - CROSS_FIRST[0])
        return slice(first_tap, first_tap + PART)

    def cross_copy(u):
        return remote(grad.at[core, part(u), depth, 1 - cross], cross_in.at[part(u)],
                      cross_sems.at[0, u], cross_sems.at[1, u], over)

    def wide_copy(u, n):
        target = (depth + slices[n]) % ring
        return remote(grad.at[core, part(u), target, 1 - cross], wide_in.at[wide_part(u), n],
                      wide_sems.at[0, u - CROSS_FIRST[0], n],
                      wide_sems.at[1, u - CROSS_FIRST[0], n], over)

    def add_wide(u, n):
        wide_copy(u, n).wait_recv()
        target = (depth + slices[n]) % ring
        grad[core, part(u), target, cross] += wide_in[wide_part(u), n]

    fine(coarse + 1, 0)
    fine(coarse + 1, 2)
    early = RING_FIRST[:1] + CROSS_FIRST
    for u in early:
        core_copy(u).start()
    fine(coarse + 1, 1)
    fine(coarse + 1, 3)
    for u in RING_FIRST[1:]:
        core_copy(u).start()
    outs = [load(image(low, i), lower_hbm.at[i], out_sems.at[i]) for i in range(2)]

    for u in early + RING_FIRST[1:]:
        core_copy(u).wait_recv()
        grad[core, part(u)] += core_in[part(u)]
        if u in CROSS_FIRST:
            for n in range(ring):
                wide_copy(u, n).start()
        else:
            ring_round(0, (u,))
    ring_round(1, RING_FIRST)
    ring_round(0, CROSS_FIRST)
    for j in range(2, half + 1):
        ring_round(j, RING_FIRST)
        if j == half:
            for u in RING_FIRST:
                cross_copy(u).start()
        ring_round(j - 1, CROSS_FIRST)
    for u in range(parts):
        core_copy(u).wait_send()
        if u in CROSS_FIRST:
            for n in range(ring):
                wide_copy(u, n).wait_send()
        for j in range(half):
            for way in range(2):
                if carries(way, j, u) and (u in RING_FIRST or j < half - 1):
                    ring_copy(way, j, u).wait_send()
    for copy in outs:
        copy.wait()

    @pl.loop(0, Q * coarse)
    def _(k):
        @pl.when((s > 0) & sends(R * k, R, h))
        def _():
            sent_chunk(k, R * k, R)

    for i in range(BLK):
        @pl.when((s > 0) & sends(BLK * coarse + i, 1, h))
        def _():
            sent_chunk(Q * coarse + i, BLK * coarse + i, 1)

    ring_round(half, CROSS_FIRST)
    for u in CROSS_FIRST:
        result[part(u)] = grad[core, part(u), depth, cross] * scale
    for u in RING_FIRST:
        cross_copy(u).wait_recv()
        result[part(u)] = (grad[core, part(u), depth, cross] + cross_in[part(u)]) * scale
    outs = [load(result, grad_hbm, out_sems.at[2])]

    for u in range(parts):
        if u in CROSS_FIRST:
            for way in range(2):
                ring_copy(way, half - 1, u).wait_send()
        else:
            cross_copy(u).wait_send()
    for copy in outs:
        copy.wait()


def on_device(states, slopes, kernels, guess):
    layers, images, height, width, chans = states.shape
    sections = lax.axis_size("layer")
    replicas = lax.axis_size("dp")
    scale = STEP / (images * replicas)
    pix = height * width
    flat = lambda array: array.reshape(layers, images, pix, chans)
    steps = Q * (2 * height // BLK) + BLK
    size = ROWS * width
    any_space = pl.BlockSpec(memory_space=pl.ANY)
    f32, bf16 = jnp.float32, jnp.bfloat16
    ring = replicas // 4
    share = chans // replicas
    lower, grads = pl.pallas_call(
        functools.partial(chain_kernel, sections, scale, height, width, chans),
        out_shape=(
            pltpu.VMEM((images, pix, chans), f32),
            pltpu.VMEM((layers * 9, chans // replicas, chans), f32),
        ),
        in_specs=[any_space] * 4,
        out_specs=(pl.BlockSpec(memory_space=pltpu.VMEM),) * 2,
        scratch_shapes=[
            pltpu.VMEM((layers, size, chans), bf16),
            pltpu.VMEM((layers, size, chans), bf16),
            pltpu.VMEM((layers, 9, chans, chans), bf16),
            pltpu.VMEM((layers, 3, 3 * chans, chans), bf16),
            pltpu.VMEM((size, chans), f32),
            pltpu.VMEM((size, chans), f32),
            pltpu.VMEM((size, chans), f32),
            pltpu.VMEM((size, chans), f32),
            pltpu.VMEM((size, chans), f32),
            pltpu.VMEM((size, chans), f32),
            pltpu.VMEM((size, 3 * chans), bf16),
            pltpu.VMEM((size, 3 * chans), bf16),
            pltpu.VMEM((size, 3 * chans), bf16),
            pltpu.VMEM((2, layers * 9, ring, 2, share, chans), f32),
            pltpu.VMEM((layers * 9, ring, 2, share, chans), f32),
            pltpu.VMEM((2, ring // 2, layers * 9, 2, share, chans), f32),
            pltpu.VMEM((layers * 9, share, chans), f32),
            pltpu.VMEM((len(CROSS_FIRST) * PART, ring, share, chans), f32),
            pltpu.VMEM((layers * 9, share, chans), f32),
            pltpu.SemaphoreType.DMA((14,)),
            pltpu.SemaphoreType.DMA((steps,)),
            pltpu.SemaphoreType.DMA((steps,)),
            pltpu.SemaphoreType.DMA((3,)),
            pltpu.SemaphoreType.DMA((2, layers * 9 // PART)),
            pltpu.SemaphoreType.DMA((2, ring // 2, layers * 9 // PART)),
            pltpu.SemaphoreType.DMA((2, ring // 2, layers * 9 // PART)),
            pltpu.SemaphoreType.DMA((2, layers * 9 // PART)),
            pltpu.SemaphoreType.DMA((2, len(CROSS_FIRST), ring)),
        ],
        compiler_params=pltpu.CompilerParams(
            collective_id=0, has_side_effects=True, vmem_limit_bytes=60 * 1024 * 1024
        ),
    )(flat(states), flat(slopes), kernels, flat(guess))
    return (
        lower.reshape(1, images, height, width, chans),
        grads.reshape(layers, 9, share, chans),
    )


def solution(mesh):
    return jax.shard_map(
        on_device,
        mesh=mesh,
        in_specs=(
            P("layer", "dp", None, None, None),
            P("layer", "dp", None, None, None),
            P("layer", None, None, None),
            P("layer", "dp", None, None, None),
        ),
        out_specs=(P("layer", "dp", None, None, None), P("layer", None, "dp", None)),
        check_vma=False,
    )
```

```python
import functools

import jax
import jax.numpy as jnp
from jax import lax
from jax.experimental import pallas as pl
from jax.experimental.pallas import tpu as pltpu
from jax.sharding import PartitionSpec as P

MESH = pl.DeviceIdType.MESH
STEP = 0.5
TOP = 8
ROWS = 88
R = 2
Q = 4
BLK = R * Q
PART = 3
RING_FIRST = (3, 0, 1, 2)
CROSS_FIRST = (4, 5)


def chain_kernel(
    sections, scale, height, width, chans,
    states_hbm, slopes_hbm, kernels_hbm, guess_hbm,
    lower_hbm, grad_hbm,
    states, slopes, kern, kern_t, last, ends, recv, send, mid, low, z_chain, z_up, z_dn, grad,
    core_in, ring_in, cross_in, wide_in, result,
    load_sems, send_sems, recv_sems, out_sems,
    core_sems, ring_send, ring_recv, cross_sems, wide_sems,
):
    s = lax.axis_index("layer")
    h = sections - 1 - s
    pix = height * width
    image_row = (1, height + 2)
    end_row = 2 * height + 1

    def rows(start, count):
        return pl.ds(pl.multiple_of((start + TOP) * width, width), count * width)

    def image(ref, i):
        return ref.at[rows(image_row[i], height)]

    def load(src, dst, sem):
        copy = pltpu.make_async_copy(src, dst, sem)
        copy.start()
        return copy

    pads = ((-TOP, TOP + 1), (height + 1, 1), (end_row + 1, ROWS - TOP - end_row - 1))

    def clear(ref):
        for start, count in pads:
            part = ref.at[rows(start, count)]
            part[...] = jnp.zeros(part.shape, part.dtype)

    def load_bottom(i):
        return [
            load(guess_hbm.at[0, i], image(ends, i), load_sems.at[1 + i]),
            load(slopes_hbm.at[0, i], image(slopes.at[0], i), load_sems.at[3 + i]),
        ]

    first = [load(kernels_hbm.at[0], kern.at[0], load_sems.at[0])] + load_bottom(0)
    place = lax.axis_index("dp")
    ring = lax.axis_size("dp") // 4
    depth = place // 4
    cross = (place // 2) % 2
    core = place % 2
    beside = place + 1 - 2 * core
    over = place + 2 - 4 * cross
    after = ((depth + 1) % ring) * 4 + place % 4
    before = ((depth + ring - 1) % ring) * 4 + place % 4

    clear(recv)
    barrier = pltpu.get_barrier_semaphore()
    for peer in (beside, over, after, before):
        pl.semaphore_signal(barrier, inc=1, device_id={"dp": peer}, device_id_type=MESH)

    @pl.when(s > 0)
    def _():
        pl.semaphore_signal(barrier, inc=1, device_id={"layer": s - 1}, device_id_type=MESH)

    @pl.when(s < sections - 1)
    def _():
        pl.semaphore_signal(barrier, inc=1, device_id={"layer": s + 1}, device_id_type=MESH)

    clear(ends)
    clear(slopes.at[0])
    clear(z_chain)

    def clear_rest():
        for ref in (last, slopes.at[1], states.at[0], states.at[1], z_up, z_dn):
            clear(ref)
        top = rows(-TOP, TOP + 4)
        z_up[top] = jnp.zeros(((TOP + 4) * width, 3 * chans), jnp.bfloat16)
        z_dn[top] = jnp.zeros(((TOP + 4) * width, 3 * chans), jnp.bfloat16)
        grad[...] = jnp.zeros(grad.shape, jnp.float32)

    @pl.when(h > 0)
    def _():
        clear_rest()

    for copy in first:
        copy.wait()
    second = load_bottom(1)
    rest = [load(kernels_hbm.at[1], kern.at[1], load_sems.at[5])]
    for i in range(2):
        rest.append(load(guess_hbm.at[1, i], image(last, i), load_sems.at[6 + i]))
        rest.append(load(slopes_hbm.at[1, i], image(slopes.at[1], i), load_sems.at[8 + i]))
        for l in range(2):
            rest.append(load(states_hbm.at[l, i], image(states.at[l], i), load_sems.at[10 + 2 * l + i]))

    def spread(z, start, count, slope, values):
        cot = slope.astype(jnp.float32) * values
        size = count * width
        col = lax.broadcasted_iota(jnp.int32, (size, chans), 0) % width
        z[rows(start, count), chans:2 * chans] = cot.astype(jnp.bfloat16)
        ahead = jnp.where(col == width - 1, 0.0, pltpu.roll(cot, size - 1, 0))
        z[rows(start, count), 0:chans] = ahead.astype(jnp.bfloat16)
        behind = jnp.where(col == 0, 0.0, pltpu.roll(cot, 1, 0))
        z[rows(start, count), 2 * chans:3 * chans] = behind.astype(jnp.bfloat16)

    def conv(z, layer, start, count):
        total = None
        for a in range(3):
            term = jnp.dot(z[rows(start + 1 - a, count), :], kern_t[layer, a],
                           preferred_element_type=jnp.float32)
            total = term if total is None else total + term
        return total

    def conv_unturned(z, start, count):
        total = None
        for a in range(3):
            for b in range(3):
                term = lax.dot_general(
                    z[rows(start + 1 - a, count), b * chans:(b + 1) * chans],
                    kern[0, 3 * a + b], (((1,), (1,)), ((), ())),
                    preferred_element_type=jnp.float32,
                )
                total = term if total is None else total + term
        return total

    def turn(layer):
        for a in range(3):
            for b in range(3):
                kern_t[layer, a, b * chans:(b + 1) * chans] = kern[layer, 3 * a + b].T

    def sends(base, size, hop):
        start = base + 1 - hop
        return (start + size - 1 >= 1) & (start <= end_row)

    def chunk(src, k, start, size):
        where = rows(start, size)
        return pltpu.make_async_remote_copy(
            src_ref=src.at[where],
            dst_ref=recv.at[where],
            send_sem=send_sems.at[k],
            recv_sem=recv_sems.at[k],
            device_id={"layer": s - 1},
            device_id_type=MESH,
        )

    def each_chunk(start, size, act):
        if size == 1:
            act(start, 1)
            return
        skip_first = (start == 0) | (start == height + 1)
        skip_last = start == height

        @pl.when(jnp.logical_not(skip_first | skip_last))
        def _():
            act(start, size)

        @pl.when(skip_first)
        def _():
            act(start + 1, size - 1)

        @pl.when(skip_last)
        def _():
            act(start, size - 1)

    def start_chunk(src, k, base, size):
        each_chunk(base + 1 - h, size, lambda at, count: chunk(src, k, at, count).start())

    def sent_chunk(k, base, size):
        each_chunk(base + 1 - h, size, lambda at, count: chunk(send, k, at, count).wait_send())

    def arrived_chunk(k, base, size):
        each_chunk(base + 2 - h, size, lambda at, count: chunk(recv, k, at, count).wait_recv())

    def spread_end(j):
        at = rows(BLK * j, BLK)
        spread(z_chain, BLK * j, BLK, slopes[0, at], ends[at])

    blocks = -(-(end_row + 1) // BLK)
    coarse = (end_row - 1) // BLK
    spread_end(0)

    @pl.loop(0, blocks)
    def _(j):
        @pl.when(j == image_row[1] // BLK - 1)
        def _():
            for copy in second:
                copy.wait()

        @pl.when(j < blocks - 1)
        def _():
            spread_end(j + 1)

        at = rows(BLK * j, BLK)
        ends[at] = ends[at] + STEP * conv_unturned(z_chain, BLK * j, BLK)

        @pl.when(j == 0)
        def _():
            peers = 4 + jnp.where(s > 0, 1, 0) + jnp.where(s < sections - 1, 1, 0)
            pl.semaphore_wait(barrier, peers)

        @pl.when((h == 0) & (s > 0))
        def _():
            for q in range(Q):
                k = Q * j - 1 + q

                @pl.when((k >= 0) & (k < Q * coarse))
                def _():
                    start_chunk(ends, k, R * k, R)

    @pl.when((h == 0) & (s > 0))
    def _():
        start_chunk(ends, Q * coarse, BLK * coarse, 1)

    @pl.when(h == 0)
    def _():
        clear_rest()

    turn(0)
    for copy in rest:
        copy.wait()

    @pl.when(h == 0)
    def _():
        for i in range(2):
            at = rows(image_row[i], height)
            recv[at] = last[at]

    def fine(j, piece):
        start = BLK * (j - 1) + 2 - jnp.maximum(h, 1)

        def gradient(layer, z, at):
            lhs = jnp.concatenate(
                [states[layer, rows(at + a - 1, BLK)].T for a in range(3)], axis=0
            )
            for b in range(3):
                term = jnp.dot(lhs, z[rows(at, BLK), b * chans:(b + 1) * chans],
                               preferred_element_type=jnp.float32)
                for a in range(3):
                    part = term[a * chans:(a + 1) * chans]
                    part = part.reshape(grad.shape[2:4] + (2,) + grad.shape[4:])
                    for c in range(2):
                        grad[c, 9 * layer + 3 * a + b] += part[:, :, c]

        if piece == 0:
            at = rows(start, BLK)
            spread(z_up, start, BLK, slopes[1, at], recv[at])
            at = rows(start - 1, BLK)
            mid[at] = recv[at] + STEP * conv(z_up, 1, start - 1, BLK)
        elif piece == 1:
            at = rows(start - 1, BLK)
            spread(z_dn, start - 1, BLK, slopes[0, at], mid[at])
            at = rows(start - 2, BLK + 1)
            low[at] = mid[at] + STEP * conv(z_dn, 0, start - 2, BLK + 1)
        elif piece == 2:
            gradient(1, z_up, start)
        else:
            gradient(0, z_dn, start - 1)

    def step(k, base, size):
        taken = (h > 0) & sends(base, size, h - 1)

        @pl.when(taken)
        def _():
            arrived_chunk(k, base, size)

        @pl.when(taken & (s > 0))
        def _():
            at = rows(base + 2 - h, size)
            spread(z_chain, base + 2 - h, size, slopes[0, at], recv[at] - last[at])

        @pl.when((h > 0) & (s > 0) & sends(base, size, h))
        def _():
            at = rows(base + 1 - h, size)
            send[at] = ((recv[at] - last[at]) + 2 * STEP * conv(z_chain, 0, base + 1 - h, size)) + ends[at]
            start_chunk(send, k, base, size)

    @pl.loop(0, coarse)
    def _(j):
        for q in range(Q):
            step(Q * j + q, BLK * j + R * q, R)

            @pl.when(j > 0)
            def _():
                fine(j, q)

        @pl.when(j == 0)
        def _():
            turn(1)

    for i in range(BLK):
        step(Q * coarse + i, BLK * coarse + i, 1)
        if i % 2 == 1:
            fine(coarse, i // 2)

    def remote(src, dst, send_sem, recv_sem, peer):
        return pltpu.make_async_remote_copy(
            src_ref=src, dst_ref=dst, send_sem=send_sem, recv_sem=recv_sem,
            device_id={"dp": peer}, device_id_type=MESH,
        )

    def part(u):
        return slice(PART * u, PART * (u + 1))

    parts = grad.shape[1] // PART
    half = ring // 2
    slices = [half] + [sign * away for away in range(half - 1, 0, -1) for sign in (1, -1)] + [0]

    def core_copy(u):
        return remote(grad.at[1 - core, part(u)], core_in.at[part(u)],
                      core_sems.at[0, u], core_sems.at[1, u], beside)

    def ring_target(way, away):
        return (depth + away) % ring if way == 0 else (depth + ring - away) % ring

    def carries(way, j, u):
        return u in RING_FIRST or j > 0 or way == u % 2

    def ring_copy(way, j, u):
        target = ring_target(way, half - j)
        if u in CROSS_FIRST:
            src, dst = grad.at[core, part(u), target, cross], ring_in.at[way, j, part(u), 0]
        elif j == 0:
            src, dst = grad.at[core, part(u), target, way], ring_in.at[way, j, part(u), way]
        else:
            src, dst = grad.at[core, part(u), target], ring_in.at[way, j, part(u)]
        return remote(src, dst, ring_send.at[way, j, u], ring_recv.at[way, j, u],
                      after if way == 0 else before)

    def add_arrived(way, j, u):
        if not carries(way, j, u):
            return
        ring_copy(way, j, u).wait_recv()
        target = ring_target(way, half - 1 - j)
        if u in CROSS_FIRST:
            grad[core, part(u), target, cross] += ring_in[way, j, part(u), 0]
        elif j == 0:
            grad[core, part(u), target, way] += ring_in[way, j, part(u), way]
        else:
            grad[core, part(u), target] += ring_in[way, j, part(u)]

    def ring_round(j, pieces):
        for u in pieces:
            if u in CROSS_FIRST:
                for n, away in enumerate(slices):
                    if abs(away) == half - j:
                        add_wide(u, n)
            for way in range(2):
                if j > 0:
                    add_arrived(way, j - 1, u)
                if j < half and carries(way, j, u):
                    ring_copy(way, j, u).start()

    def wide_part(u):
        first_tap = PART * (u - CROSS_FIRST[0])
        return slice(first_tap, first_tap + PART)

    def cross_copy(u):
        return remote(grad.at[core, part(u), depth, 1 - cross], cross_in.at[part(u)],
                      cross_sems.at[0, u], cross_sems.at[1, u], over)

    def wide_copy(u, n):
        target = (depth + slices[n]) % ring
        return remote(grad.at[core, part(u), target, 1 - cross], wide_in.at[wide_part(u), n],
                      wide_sems.at[0, u - CROSS_FIRST[0], n],
                      wide_sems.at[1, u - CROSS_FIRST[0], n], over)

    def add_wide(u, n):
        wide_copy(u, n).wait_recv()
        target = (depth + slices[n]) % ring
        grad[core, part(u), target, cross] += wide_in[wide_part(u), n]

    fine(coarse + 1, 0)
    fine(coarse + 1, 2)
    early = RING_FIRST[:1] + CROSS_FIRST
    for u in early:
        core_copy(u).start()
    fine(coarse + 1, 1)
    fine(coarse + 1, 3)
    for u in RING_FIRST[1:]:
        core_copy(u).start()
    outs = [load(image(low, i), lower_hbm.at[i], out_sems.at[i]) for i in range(2)]

    for u in early + RING_FIRST[1:]:
        core_copy(u).wait_recv()
        grad[core, part(u)] += core_in[part(u)]
        if u in CROSS_FIRST:
            for n in range(ring):
                wide_copy(u, n).start()
        else:
            ring_round(0, (u,))
    ring_round(1, RING_FIRST)
    ring_round(0, CROSS_FIRST)
    for j in range(2, half + 1):
        ring_round(j, RING_FIRST)
        if j == half:
            for u in RING_FIRST:
                cross_copy(u).start()
        ring_round(j - 1, CROSS_FIRST)
    for u in range(parts):
        core_copy(u).wait_send()
        if u in CROSS_FIRST:
            for n in range(ring):
                wide_copy(u, n).wait_send()
        for j in range(half):
            for way in range(2):
                if carries(way, j, u) and (u in RING_FIRST or j < half - 1):
                    ring_copy(way, j, u).wait_send()
    for copy in outs:
        copy.wait()

    @pl.loop(0, Q * coarse)
    def _(k):
        @pl.when((s > 0) & sends(R * k, R, h))
        def _():
            sent_chunk(k, R * k, R)

    for i in range(BLK):
        @pl.when((s > 0) & sends(BLK * coarse + i, 1, h))
        def _():
            sent_chunk(Q * coarse + i, BLK * coarse + i, 1)

    ring_round(half, CROSS_FIRST)
    for u in CROSS_FIRST:
        result[part(u)] = grad[core, part(u), depth, cross] * scale
    for u in RING_FIRST:
        cross_copy(u).wait_recv()
        result[part(u)] = (grad[core, part(u), depth, cross] + cross_in[part(u)]) * scale
    outs = [load(result, grad_hbm, out_sems.at[2])]

    for u in range(parts):
        if u in CROSS_FIRST:
            for way in range(2):
                ring_copy(way, half - 1, u).wait_send()
        else:
            cross_copy(u).wait_send()
    for copy in outs:
        copy.wait()


def on_device(states, slopes, kernels, guess):
    layers, images, height, width, chans = states.shape
    sections = lax.axis_size("layer")
    replicas = lax.axis_size("dp")
    scale = STEP / (images * replicas)
    pix = height * width
    flat = lambda array: array.reshape(layers, images, pix, chans)
    steps = Q * (2 * height // BLK) + BLK
    size = ROWS * width
    any_space = pl.BlockSpec(memory_space=pl.ANY)
    f32, bf16 = jnp.float32, jnp.bfloat16
    ring = replicas // 4
    share = chans // replicas
    lower, grads = pl.pallas_call(
        functools.partial(chain_kernel, sections, scale, height, width, chans),
        out_shape=(
            pltpu.VMEM((images, pix, chans), f32),
            pltpu.VMEM((layers * 9, chans // replicas, chans), f32),
        ),
        in_specs=[any_space] * 4,
        out_specs=(pl.BlockSpec(memory_space=pltpu.VMEM),) * 2,
        scratch_shapes=[
            pltpu.VMEM((layers, size, chans), bf16),
            pltpu.VMEM((layers, size, chans), bf16),
            pltpu.VMEM((layers, 9, chans, chans), bf16),
            pltpu.VMEM((layers, 3, 3 * chans, chans), bf16),
            pltpu.VMEM((size, chans), f32),
            pltpu.VMEM((size, chans), f32),
            pltpu.VMEM((size, chans), f32),
            pltpu.VMEM((size, chans), f32),
            pltpu.VMEM((size, chans), f32),
            pltpu.VMEM((size, chans), f32),
            pltpu.VMEM((size, 3 * chans), bf16),
            pltpu.VMEM((size, 3 * chans), bf16),
            pltpu.VMEM((size, 3 * chans), bf16),
            pltpu.VMEM((2, layers * 9, ring, 2, share, chans), f32),
            pltpu.VMEM((layers * 9, ring, 2, share, chans), f32),
            pltpu.VMEM((2, ring // 2, layers * 9, 2, share, chans), f32),
            pltpu.VMEM((layers * 9, share, chans), f32),
            pltpu.VMEM((len(CROSS_FIRST) * PART, ring, share, chans), f32),
            pltpu.VMEM((layers * 9, share, chans), f32),
            pltpu.SemaphoreType.DMA((14,)),
            pltpu.SemaphoreType.DMA((steps,)),
            pltpu.SemaphoreType.DMA((steps,)),
            pltpu.SemaphoreType.DMA((3,)),
            pltpu.SemaphoreType.DMA((2, layers * 9 // PART)),
            pltpu.SemaphoreType.DMA((2, ring // 2, layers * 9 // PART)),
            pltpu.SemaphoreType.DMA((2, ring // 2, layers * 9 // PART)),
            pltpu.SemaphoreType.DMA((2, layers * 9 // PART)),
            pltpu.SemaphoreType.DMA((2, len(CROSS_FIRST), ring)),
        ],
        compiler_params=pltpu.CompilerParams(
            collective_id=0, has_side_effects=True, vmem_limit_bytes=60 * 1024 * 1024
        ),
    )(flat(states), flat(slopes), kernels, flat(guess))
    return (
        lower.reshape(1, images, height, width, chans),
        grads.reshape(layers, 9, share, chans),
    )


def solution(mesh):
    return jax.shard_map(
        on_device,
        mesh=mesh,
        in_specs=(
            P("layer", "dp", None, None, None),
            P("layer", "dp", None, None, None),
            P("layer", None, None, None),
            P("layer", "dp", None, None, None),
        ),
        out_specs=(P("layer", "dp", None, None, None), P("layer", None, "dp", None)),
        check_vma=False,
    )
```
